256 devices in a mesh: inner: 32 (over z, y_hi, core), outer: 8 (over y_lo, x).
Axes of the slice: x: 4, y: 4 (y_hi: 2, y_lo: 2; y = y_hi * 2 + y_lo), z: 8, core: 2. Of those that a mesh axis runs over, the one named last changes fastest.
Arguments:
- queries: bfloat16 [32768, 1024], P(('outer', 'inner')), may hold values from -8 to 8
- key_rows: bfloat16 [32768, 128], P(('outer', 'inner')), may hold values from -8 to 8
- value_rows: bfloat16 [32768, 128], P(('outer', 'inner')), may hold values from -6 to 6
- grad_output: bfloat16 [32768, 1024], P(('outer', 'inner')), may hold values from -6 to 6
- doc_blocks: int32 [256], replicated, may hold values from 0 to 31, never falling along the last dimension, each value on 1 to 32 neighbouring positions
Outputs:
- grad_queries: bfloat16 [32768, 1024], P(('outer', 'inner'))
- grad_keys: bfloat16 [32768, 128], P(('outer', 'inner'))
- grad_values: bfloat16 [32768, 128], P(('outer', 'inner'))
The draws below stay inside these ranges and needn't reach their ends.
All inputs are finite; a program needn't handle non-finite values.
Results may differ from the reference program's by a relative error of at most 0.019.
Values may be sent and summed in bfloat16 or wider, within the bound.
A program may use at most 64 MiB of HBM per device.

```python
import math
import jax
import jax.numpy as jnp
import numpy as np
from jax import lax

DH = 128
HEADS = 8
BLK = 128
NBLK = 256
SEQ = 32768
DOCBLK = 32


def draw_queries(key, part):
    return jnp.clip(jax.random.normal(jax.random.fold_in(key, 5), (SEQ, HEADS * DH), jnp.float32), -4.0, 4.0).astype(jnp.bfloat16)


def draw_key_rows(key, part):
    return jnp.clip(jax.random.normal(jax.random.fold_in(key, 6), (SEQ, DH), jnp.float32), -4.0, 4.0).astype(jnp.bfloat16)


def levels(own_key, shape, split, low, largest):
    loudness = 1.0
    for position, shards_of in split:
        draws = jax.random.uniform(jax.random.fold_in(jax.random.fold_in(own_key, 6), position), (shards_of,), jnp.float32, low / len(split), largest / len(split))
        loudness = loudness * jnp.repeat(jnp.exp(draws), shape[position] // shards_of).reshape((-1,) + (1,) * (len(shape) - 1 - position))
    return loudness


def length_profile(number_of, total, reach, slope):
    weights = [(1 << 20) // math.isqrt(rank ** slope) + 1 for rank in range(2, number_of + 1)]
    rest, counts = total - reach - (number_of - 1), [1] * (number_of - 1)
    while rest > 0:
        candidates = [i for i in range(number_of - 1) if counts[i] < reach]
        whole, remaining = sum([weights[i] for i in candidates]), rest
        for i in candidates:
            addition = min(reach - counts[i], max(1, remaining * weights[i] // whole), rest)
            counts[i] = counts[i] + addition
            rest = rest - addition
    return np.array([reach] + counts)


def ragged(rng, count, total, reach, lean):
    if count == 2:
        one = jax.random.randint(rng, (), max(1, total - reach), min(reach, total - 1) + 1)
        return jnp.stack([one, total - one])
    lengths = jnp.asarray(length_profile(count, total, reach, lean), jnp.int32)
    couples = (count - 1) // 2
    giver, receiver = lengths[1:1 + 2 * couples:2], lengths[2:2 + 2 * couples:2]
    margin = jnp.minimum(giver - 1, reach - receiver)
    moved = jax.random.randint(jax.random.fold_in(rng, 1), (couples,), 0, 1 << 20) % (margin + 1)
    lengths = lengths.at[1:1 + 2 * couples:2].set(giver - moved).at[2:2 + 2 * couples:2].set(receiver + moved)
    return lengths[jax.random.permutation(jax.random.fold_in(rng, 2), count)]


def noise(key, shape, scale, limit, cuts=(), kind=jnp.bfloat16):
    entries = scale * jax.random.normal(key, shape, jnp.float32)
    if cuts:
        entries = entries * levels(key, shape, cuts, -0.22, 0.18)
    return jnp.clip(entries, -limit, limit).astype(kind)


def setup_inputs(seed: int = 0) -> dict:
    key_of = jax.random.split(jax.random.key(seed), 6)
    queries = draw_queries(jax.random.fold_in(key_of[5], 71), 0)
    key_rows = draw_key_rows(jax.random.fold_in(key_of[5], 71), 0)
    value_rows = noise(key_of[2], (SEQ, DH), 1.0, 6.0, ((0, 256),))
    grad_output = noise(key_of[3], (SEQ, HEADS * DH), 1.0, 6.0, ((0, 256),))
    doc_blocks = jnp.searchsorted(jnp.cumsum(ragged(key_of[4], NBLK // 8, NBLK, DOCBLK, 2)), jnp.arange(NBLK), side="right").astype(jnp.int32)
    return {"queries": queries, "key_rows": key_rows, "value_rows": value_rows, "grad_output": grad_output, "doc_blocks": doc_blocks}


def reference(queries, key_rows, value_rows, grad_output, doc_blocks):
    scaling = DH ** -0.5
    span = DOCBLK * BLK
    keys_pad = jnp.concatenate([jnp.zeros((span, DH), key_rows.dtype), key_rows], axis=0)
    values_pad = jnp.concatenate([jnp.zeros((span, DH), value_rows.dtype), value_rows], axis=0)
    docs_pad = jnp.concatenate([jnp.full((DOCBLK,), -1, jnp.int32), doc_blocks.astype(jnp.int32)])
    query_blocks = queries.reshape(NBLK, BLK, HEADS, DH)
    grad_blocks = grad_output.reshape(NBLK, BLK, HEADS, DH)
    key_pos = jnp.arange(span, dtype=jnp.int32)
    query_pos = span - BLK + jnp.arange(BLK, dtype=jnp.int32)

    def step(running, block_index):
        grad_k, grad_v = running
        first = ((block_index + 1) * BLK).astype(jnp.int32)
        key_win = lax.dynamic_slice_in_dim(keys_pad, first, span, 0).astype(jnp.float32)
        value_win = lax.dynamic_slice_in_dim(values_pad, first, span, 0).astype(jnp.float32)
        tags = lax.dynamic_slice_in_dim(docs_pad, (block_index + 1).astype(jnp.int32), DOCBLK, 0)
        key_tags = jnp.repeat(tags, BLK)
        own_tag = lax.dynamic_index_in_dim(doc_blocks, block_index, 0, keepdims=False)
        allowed = (key_tags[None, :] == own_tag) & (key_pos[None, :] <= query_pos[:, None])
        allowed = allowed[:, None, :]
        query_here = lax.dynamic_index_in_dim(query_blocks, block_index, 0, keepdims=False).astype(jnp.float32)
        grad_here = lax.dynamic_index_in_dim(grad_blocks, block_index, 0, keepdims=False).astype(jnp.float32)
        scores = jnp.einsum('thd,kd->thk', query_here, key_win) * scaling
        row_max = jnp.max(jnp.where(allowed, scores, -jnp.inf), axis=-1, keepdims=True)
        weights = jnp.exp(jnp.where(allowed, scores - row_max, -jnp.inf))
        row_sum = jnp.sum(weights, axis=-1, keepdims=True)
        probs = weights / row_sum
        attn_out = jnp.einsum('thk,kd->thd', probs, value_win, precision=lax.Precision.HIGHEST)
        delta = jnp.sum(grad_here * attn_out, axis=-1, keepdims=True)
        probs_low = probs.astype(jnp.bfloat16).astype(jnp.float32)
        value_part = jnp.einsum('thk,thd->kd', probs_low, grad_here)
        dprobs = jnp.einsum('thd,kd->thk', grad_here, value_win)
        dscores = (probs * (dprobs - delta) * scaling).astype(jnp.bfloat16).astype(jnp.float32)
        grad_q = jnp.einsum('thk,kd->thd', dscores, key_win).astype(jnp.bfloat16)
        key_part = jnp.einsum('thk,thd->kd', dscores, query_here)
        grad_k = lax.dynamic_update_slice_in_dim(grad_k, lax.dynamic_slice_in_dim(grad_k, first, span, 0) + key_part, first, 0)
        grad_v = lax.dynamic_update_slice_in_dim(grad_v, lax.dynamic_slice_in_dim(grad_v, first, span, 0) + value_part, first, 0)
        return (grad_k, grad_v), grad_q

    start_state = (jnp.zeros((SEQ + span, DH), jnp.float32), jnp.zeros((SEQ + span, DH), jnp.float32))
    (grad_k, grad_v), grad_q = lax.scan(step, start_state, jnp.arange(NBLK, dtype=jnp.int32))
    grad_queries = grad_q.reshape(SEQ, HEADS * DH)
    return grad_queries, grad_k[span:].astype(jnp.bfloat16), grad_v[span:].astype(jnp.bfloat16)
```

```python
import functools
import math

import jax
import jax.numpy as jnp
from jax import lax
from jax.experimental import pallas as pl
from jax.experimental.pallas import tpu as pltpu
from jax.sharding import PartitionSpec as P

MESH = pl.DeviceIdType.MESH
WINDOW = 16
LINE = WINDOW // 2
SLOTS = WINDOW + 1
COLS = 256
LOW = -1e30
HIGH = 3e38


def nearest(n):
    n = n + 1
    half = n // 2
    k = half + (n % 2) * (LINE - 2 * half)
    return jnp.where(k == 0, LINE, k)


def farthest(n):
    return nearest(LINE - 1 - n)


def kernel(
    inner_count,
    chips,
    blk,
    width,
    heads,
    q_ref,
    k_ref,
    v_ref,
    do_ref,
    doc_ref,
    dq_ref,
    dk_ref,
    dv_ref,
    kv,
    keys_t,
    rows_q,
    rows_do,
    cols_q,
    cols_do,
    weights,
    dprobs,
    tile_max,
    run_max,
    run_sum,
    run_dot,
    own_stats,
    other_stats,
    low,
    dsc,
    out_buf,
    from_pair,
    from_line,
    own_part,
    dq_send,
    dq_recv,
    line_send,
    line_recv,
    pair_send,
    pair_recv,
    back_pair_send,
    back_pair_recv,
    back_line_send,
    back_line_recv,
    core_send,
    core_recv,
):
    rows = heads * blk
    tiles = rows // COLS
    both = 2 * tiles
    scale = width ** (-0.5)
    scale2 = scale * math.log2(math.e)
    per_group = inner_count // 2

    outer = lax.axis_index("outer")
    inner = lax.axis_index("inner")
    core = inner % 2
    chip = outer * per_group + inner // 2
    odd = chip % 2

    def device(chip_at, core_at):
        return {
            "outer": chip_at // per_group,
            "inner": (chip_at % per_group) * 2 + core_at,
        }

    def later(k):
        return device((chip + 2 * k) % chips, core)

    def earlier(k):
        return device((chip - 2 * k + chips) % chips, core)

    other_core = device(chip, 1 - core)
    pair = device(chip + 1 - 2 * odd, core)

    def copy(src, dst, send, recv, to):
        return pltpu.make_async_remote_copy(
            src_ref=src,
            dst_ref=dst,
            send_sem=send,
            recv_sem=recv,
            device_id=to,
            device_id_type=MESH,
        )

    def line_copy(k):
        return copy(
            kv.at[0], kv.at[2 * k], line_send.at[k], line_recv.at[k], later(k)
        )

    def pair_copy(m):
        b = m + 1 - odd
        return copy(
            kv.at[2 * m], kv.at[2 * b - 1], pair_send.at[b], pair_recv.at[b], pair
        )

    def pair_arrival(b):
        return copy(
            kv.at[0], kv.at[2 * b - 1], pair_send.at[b], pair_recv.at[b], pair
        )

    def back_pair_copy(b):
        m = b - odd
        return copy(
            out_buf.at[2 * b - 1],
            from_pair.at[m],
            back_pair_send.at[m],
            back_pair_recv.at[m],
            pair,
        )

    def back_pair_arrival(m):
        return copy(
            out_buf.at[0],
            from_pair.at[m],
            back_pair_send.at[m],
            back_pair_recv.at[m],
            pair,
        )

    def back_line_copy(k):
        return copy(
            out_buf.at[2 * k],
            from_line.at[k],
            back_line_send.at[k],
            back_line_recv.at[k],
            earlier(k),
        )

    def core_copies():
        own = pl.ds(pl.multiple_of(core * rows, rows), rows)
        return (
            copy(
                rows_q.at[own], rows_q.at[own], core_send.at[0], core_recv.at[0],
                other_core,
            ),
            copy(
                rows_do.at[own], rows_do.at[own], core_send.at[1], core_recv.at[1],
                other_core,
            ),
        )

    def core_arrivals():
        own = pl.ds(pl.multiple_of((1 - core) * rows, rows), rows)
        return (
            copy(
                rows_q.at[own], rows_q.at[own], core_send.at[0], core_recv.at[0],
                other_core,
            ),
            copy(
                rows_do.at[own], rows_do.at[own], core_send.at[1], core_recv.at[1],
                other_core,
            ),
        )

    barrier = pltpu.get_barrier_semaphore()
    for k in range(1, LINE + 1):
        for to in (later(k), earlier(k)):
            pl.semaphore_signal(barrier, inc=1, device_id=to, device_id_type=MESH)
    for to in (other_core, pair):
        pl.semaphore_signal(barrier, inc=1, device_id=to, device_id_type=MESH)

    kv[0, :, :width] = k_ref[...]
    kv[0, :, width:] = v_ref[...]
    for h in range(heads):
        at = pl.ds(pl.multiple_of(core * rows + h * blk, blk), blk)
        rows_q[at, :] = q_ref[:, h * width : (h + 1) * width]
        rows_do[at, :] = do_ref[:, h * width : (h + 1) * width]
    run_max[...] = jnp.full(run_max.shape, LOW, jnp.float32)
    run_sum[...] = jnp.zeros(run_sum.shape, jnp.float32)
    run_dot[...] = jnp.zeros(run_dot.shape, jnp.float32)

    pl.semaphore_wait(barrier, 2 * LINE + 2)

    def start_line(n, carry):
        line_copy(nearest(n)).start()
        return carry

    for c in core_copies():
        c.start()
    lax.fori_loop(0, LINE, start_line, 0)

    @pl.when(odd == 0)
    def _():
        pair_copy(0).start()

    def columns(base):
        def one(i, carry):
            at = pl.ds(pl.multiple_of(base + i * blk, blk), blk)
            cols_q[:, at] = rows_q[at, :].T
            cols_do[:, at] = rows_do[at, :].T
            return carry

        lax.fori_loop(0, heads, one, 0)

    columns(core * rows)
    for c in core_arrivals():
        c.wait_recv()
    columns((1 - core) * rows)

    def forward(slot, own):
        key_chip = (chip - slot + chips) % chips
        key_block = 2 * key_chip + core
        key_tag = doc_ref[key_block]
        key_tile = kv[slot, :, :width]
        value_tile = kv[slot, :, width:]
        keys_t[:, pl.ds(pl.multiple_of(slot * blk, blk), blk)] = key_tile.T

        def tile(i, carry):
            at = pl.ds(pl.multiple_of(i * COLS, COLS), COLS)
            query_half = i // tiles
            query_block = 2 * chip + query_half
            seen = (key_tag == doc_ref[query_block]) & (key_block <= query_block)
            s = jnp.dot(key_tile, cols_q[:, at], preferred_element_type=jnp.float32)
            dp = jnp.dot(value_tile, cols_do[:, at], preferred_element_type=jnp.float32)
            s = s * scale2
            if own:
                key_at = lax.broadcasted_iota(jnp.int32, (blk, COLS), 0)
                query_at = lax.broadcasted_iota(jnp.int32, (blk, COLS), 1) % blk
                s = jnp.where(
                    key_at - query_at <= (query_half - core) * blk, s, 2 * LOW
                )
            s3 = s.reshape(blk // 8, 8, COLS)
            dp3 = dp.reshape(blk // 8, 8, COLS)
            top = jnp.max(s3, axis=0)
            old = run_max[:, at]
            new = jnp.where(seen, jnp.maximum(old, top), old)
            used = jnp.where(seen, new, HIGH)
            w = jnp.exp2(s3 - used[None])
            factor = jnp.exp2(old - new)
            run_max[:, at] = new
            tile_max[slot, :, at] = new
            run_sum[:, at] = run_sum[:, at] * factor + jnp.sum(w, axis=0)
            run_dot[:, at] = run_dot[:, at] * factor + jnp.sum(w * dp3, axis=0)
            weights[slot, :, at] = w.reshape(blk, COLS)
            dprobs[slot, :, at] = dp
            return carry

        lax.fori_loop(0, both, tile, 0)

    forward(0, True)

    def gather_step(n, carry):
        @pl.when(n < LINE)
        def _():
            k = nearest(n)
            line_copy(k).wait_recv()

            @pl.when((k < LINE) | (odd == 1))
            def _():
                pair_copy(k).start()

            forward(2 * k, False)

        @pl.when(n > 0)
        def _():
            k = nearest(n - 1)
            b = jnp.where(odd == 1, k % LINE + 1, k)
            pair_arrival(b).wait_recv()
            forward(2 * b - 1, False)

        return carry

    lax.fori_loop(0, LINE + 1, gather_step, 0)

    m8 = run_max[...]
    m1 = jnp.max(m8, axis=0, keepdims=True)
    f8 = jnp.exp2(m8 - m1)
    own_stats[0:1, :] = m1
    own_stats[1:2, :] = jnp.sum(run_sum[...] * f8, axis=0, keepdims=True)
    own_stats[2:3, :] = jnp.sum(run_dot[...] * f8, axis=0, keepdims=True)
    stats_copy = copy(
        own_stats, other_stats, core_send.at[2], core_recv.at[2], other_core
    )
    stats_copy.start()
    stats_copy.wait()
    ma, mb = own_stats[0:1, :], other_stats[0:1, :]
    m1 = jnp.maximum(ma, mb)
    fa, fb = jnp.exp2(ma - m1), jnp.exp2(mb - m1)
    total = own_stats[1:2, :] * fa + other_stats[1:2, :] * fb
    delta = (own_stats[2:3, :] * fa + other_stats[2:3, :] * fb) / total
    run_max[...] = jnp.broadcast_to(m1, run_max.shape)
    run_sum[...] = jnp.broadcast_to(1.0 / total, run_sum.shape)
    run_dot[...] = jnp.broadcast_to(delta, run_dot.shape)

    def backward(slot):
        def tile(i, carry):
            at = pl.ds(pl.multiple_of(i * COLS, COLS), COLS)
            factor = jnp.exp2(tile_max[slot, :, at] - run_max[:, at]) * run_sum[:, at]
            p3 = weights[slot, :, at].reshape(blk // 8, 8, COLS) * factor[None]
            dp3 = dprobs[slot, :, at].reshape(blk // 8, 8, COLS)
            ds3 = p3 * (dp3 - run_dot[:, at][None])
            low[:, at] = p3.reshape(blk, COLS).astype(jnp.bfloat16)
            dsc[pl.ds(pl.multiple_of(slot * blk, blk), blk), at] = ds3.reshape(
                blk, COLS
            ).astype(jnp.bfloat16)
            return carry

        lax.fori_loop(0, both, tile, 0)
        dv = jnp.dot(low[...], rows_do[...], preferred_element_type=jnp.float32)
        dk = jnp.dot(
            dsc[pl.ds(pl.multiple_of(slot * blk, blk), blk), :],
            rows_q[...],
            preferred_element_type=jnp.float32,
        )
        return dk * scale, dv

    @pl.when(odd == 0)
    def _():
        from_pair[LINE] = jnp.zeros(from_pair.shape[1:], jnp.bfloat16)

    @pl.when(odd == 1)
    def _():
        from_pair[0] = jnp.zeros(from_pair.shape[1:], jnp.bfloat16)

    def return_step(n, carry):
        @pl.when(n < LINE)
        def _():
            k = farthest(n)
            b = jnp.where(odd == 1, k % LINE + 1, k)
            dk, dv = backward(2 * b - 1)
            out_buf[2 * b - 1, :, :width] = dk.astype(jnp.bfloat16)
            out_buf[2 * b - 1, :, width:] = dv.astype(jnp.bfloat16)
            back_pair_copy(b).start()

        @pl.when(n > 0)
        def _():
            k = farthest(n - 1)
            dk, dv = backward(2 * k)

            @pl.when((k < LINE) | (odd == 1))
            def _():
                back_pair_arrival(k).wait_recv()

            got = from_pair[k].astype(jnp.float32)
            out_buf[2 * k, :, :width] = (dk + got[:, :width]).astype(jnp.bfloat16)
            out_buf[2 * k, :, width:] = (dv + got[:, width:]).astype(jnp.bfloat16)
            back_line_copy(k).start()

        return carry

    lax.fori_loop(0, LINE + 1, return_step, 0)

    dk, dv = backward(0)
    own_part[:, :width] = dk
    own_part[:, width:] = dv

    def query_tile(i):
        at = pl.ds(pl.multiple_of(i * blk, blk), blk)
        part = jnp.dot(keys_t[...], dsc[:, at], preferred_element_type=jnp.float32)
        return (part * scale).T

    def far_rows(i, carry):
        at = pl.ds(pl.multiple_of(i * width, width), width)
        dq_send[:, at] = query_tile((1 - core) * heads + i).astype(jnp.bfloat16)
        return carry

    lax.fori_loop(0, heads, far_rows, 0)
    dq_copy = copy(dq_send, dq_recv, core_send.at[3], core_recv.at[3], other_core)
    dq_copy.start()

    def near_rows(i, carry):
        at = pl.ds(pl.multiple_of(i * width, width), width)
        near = query_tile(core * heads + i)
        dq_ref[:, at] = (near + dq_recv[:, at].astype(jnp.float32)).astype(jnp.bfloat16)
        return carry

    dq_copy.wait()
    lax.fori_loop(0, heads, near_rows, 0)

    @pl.when(odd == 0)
    def _():
        back_pair_arrival(0).wait_recv()

    own_part[...] += from_pair[0].astype(jnp.float32)

    def add_line(n, carry):
        k = farthest(n)
        back_line_copy(k).wait_recv()
        own_part[...] += from_line[k].astype(jnp.float32)
        return carry

    lax.fori_loop(0, LINE, add_line, 0)
    dk_ref[...] = own_part[:, :width].astype(jnp.bfloat16)
    dv_ref[...] = own_part[:, width:].astype(jnp.bfloat16)

    def finish(n, carry):
        k = n + 1
        line_copy(k).wait_send()
        back_line_copy(k).wait_send()
        pair_copy(n + odd).wait_send()
        back_pair_copy(k).wait_send()
        return carry

    lax.fori_loop(0, LINE, finish, 0)
    for c in core_copies():
        c.wait_send()


def solution(mesh):
    inner_count = mesh.shape["inner"]
    devices = inner_count * mesh.shape["outer"]

    def shards(queries, key_rows, value_rows, grad_output, doc_blocks):
        blk, width = key_rows.shape
        heads = queries.shape[1] // width
        rows = heads * blk
        bf16, f32 = jnp.bfloat16, jnp.float32
        vmem = pl.BlockSpec(memory_space=pltpu.VMEM)
        dma = pltpu.SemaphoreType.DMA
        return pl.pallas_call(
            functools.partial(kernel, inner_count, devices // 2, blk, width, heads),
            name="attention_backward",
            out_shape=(
                jax.ShapeDtypeStruct(queries.shape, bf16),
                jax.ShapeDtypeStruct(key_rows.shape, bf16),
                jax.ShapeDtypeStruct(value_rows.shape, bf16),
            ),
            in_specs=[vmem] * 4 + [pl.BlockSpec(memory_space=pltpu.SMEM)],
            out_specs=(vmem, vmem, vmem),
            scratch_shapes=[
                pltpu.VMEM((SLOTS, blk, 2 * width), bf16),
                pltpu.VMEM((width, SLOTS * blk), bf16),
                pltpu.VMEM((2 * rows, width), bf16),
                pltpu.VMEM((2 * rows, width), bf16),
                pltpu.VMEM((width, 2 * rows), bf16),
                pltpu.VMEM((width, 2 * rows), bf16),
                pltpu.VMEM((SLOTS, blk, 2 * rows), f32),
                pltpu.VMEM((SLOTS, blk, 2 * rows), f32),
                pltpu.VMEM((SLOTS, 8, 2 * rows), f32),
                pltpu.VMEM((8, 2 * rows), f32),
                pltpu.VMEM((8, 2 * rows), f32),
                pltpu.VMEM((8, 2 * rows), f32),
                pltpu.VMEM((3, 2 * rows), f32),
                pltpu.VMEM((3, 2 * rows), f32),
                pltpu.VMEM((blk, 2 * rows), bf16),
                pltpu.VMEM((SLOTS * blk, 2 * rows), bf16),
                pltpu.VMEM((SLOTS, blk, 2 * width), bf16),
                pltpu.VMEM((LINE + 1, blk, 2 * width), bf16),
                pltpu.VMEM((LINE + 1, blk, 2 * width), bf16),
                pltpu.VMEM((blk, 2 * width), f32),
                pltpu.VMEM((blk, heads * width), bf16),
                pltpu.VMEM((blk, heads * width), bf16),
                dma((LINE + 1,)),
                dma((LINE + 1,)),
                dma((LINE + 1,)),
                dma((LINE + 1,)),
                dma((LINE + 1,)),
                dma((LINE + 1,)),
                dma((LINE + 1,)),
                dma((LINE + 1,)),
                dma((4,)),
                dma((4,)),
            ],
            compiler_params=pltpu.CompilerParams(
                collective_id=0, has_side_effects=True, vmem_limit_bytes=60 << 20
            ),
        )(queries, key_rows, value_rows, grad_output, doc_blocks)

    rows = P(("outer", "inner"), None)
    return jax.shard_map(
        shards,
        mesh=mesh,
        in_specs=(rows, rows, rows, rows, P()),
        out_specs=(rows, rows, rows),
        check_vma=False,
    )
```

```python
import functools
import math

import jax
import jax.numpy as jnp
from jax import lax
from jax.experimental import pallas as pl
from jax.experimental.pallas import tpu as pltpu
from jax.sharding import PartitionSpec as P

MESH = pl.DeviceIdType.MESH
WINDOW = 16
LINE = WINDOW // 2
SLOTS = WINDOW + 1
COLS = 256
AHEAD = 8
LAG = 3
BACK_LAG = 3
LOW = -1e30
HIGH = 3e38


def nearest(n):
    n = n + 1
    half = n // 2
    k = half + (n % 2) * (LINE - 2 * half)
    return jnp.where(k == 0, LINE, k)


def farthest(n):
    return nearest(LINE - 1 - n)


def kernel(
    inner_count,
    chips,
    blk,
    width,
    heads,
    q_ref,
    k_ref,
    v_ref,
    do_ref,
    doc_ref,
    dq_ref,
    dk_ref,
    dv_ref,
    kv,
    keys_t,
    rows_q,
    rows_do,
    cols_q,
    cols_do,
    weights,
    dprobs,
    tile_max,
    run_max,
    run_sum,
    run_dot,
    own_stats,
    other_stats,
    low,
    dsc,
    out_buf,
    from_pair,
    from_line,
    own_part,
    near,
    dq_send,
    dq_recv,
    line_send,
    line_recv,
    pair_send,
    pair_recv,
    back_pair_send,
    back_pair_recv,
    back_line_send,
    back_line_recv,
    core_send,
    core_recv,
):
    rows = heads * blk
    tiles = rows // COLS
    both = 2 * tiles
    scale = width ** (-0.5)
    scale2 = scale * math.log2(math.e)
    per_group = inner_count // 2

    outer = lax.axis_index("outer")
    inner = lax.axis_index("inner")
    core = inner % 2
    chip = outer * per_group + inner // 2
    odd = chip % 2

    def device(chip_at, core_at):
        return {
            "outer": chip_at // per_group,
            "inner": (chip_at % per_group) * 2 + core_at,
        }

    def later(k):
        return device((chip + 2 * k) % chips, core)

    def earlier(k):
        return device((chip - 2 * k + chips) % chips, core)

    other_core = device(chip, 1 - core)
    pair = device(chip + 1 - 2 * odd, core)

    def copy(src, dst, send, recv, to):
        return pltpu.make_async_remote_copy(
            src_ref=src,
            dst_ref=dst,
            send_sem=send,
            recv_sem=recv,
            device_id=to,
            device_id_type=MESH,
        )

    def line_copy(k):
        return copy(
            kv.at[0], kv.at[2 * k], line_send.at[k], line_recv.at[k], later(k)
        )

    def pair_copy(m):
        b = m + 1 - odd
        return copy(
            kv.at[2 * m], kv.at[2 * b - 1], pair_send.at[b], pair_recv.at[b], pair
        )

    def pair_arrival(b):
        return copy(
            kv.at[0], kv.at[2 * b - 1], pair_send.at[b], pair_recv.at[b], pair
        )

    def back_pair_copy(b):
        m = b - odd
        return copy(
            out_buf.at[2 * b - 1],
            from_pair.at[m],
            back_pair_send.at[m],
            back_pair_recv.at[m],
            pair,
        )

    def back_pair_arrival(m):
        return copy(
            out_buf.at[0],
            from_pair.at[m],
            back_pair_send.at[m],
            back_pair_recv.at[m],
            pair,
        )

    def back_line_copy(k):
        return copy(
            out_buf.at[2 * k],
            from_line.at[k],
            back_line_send.at[k],
            back_line_recv.at[k],
            earlier(k),
        )

    def core_copies():
        own = pl.ds(pl.multiple_of(core * rows, rows), rows)
        return (
            copy(
                rows_q.at[own], rows_q.at[own], core_send.at[0], core_recv.at[0],
                other_core,
            ),
            copy(
                rows_do.at[own], rows_do.at[own], core_send.at[1], core_recv.at[1],
                other_core,
            ),
        )

    def core_arrivals():
        own = pl.ds(pl.multiple_of((1 - core) * rows, rows), rows)
        return (
            copy(
                rows_q.at[own], rows_q.at[own], core_send.at[0], core_recv.at[0],
                other_core,
            ),
            copy(
                rows_do.at[own], rows_do.at[own], core_send.at[1], core_recv.at[1],
                other_core,
            ),
        )

    barrier = pltpu.get_barrier_semaphore()
    for k in range(1, LINE + 1):
        for to in (later(k), earlier(k)):
            pl.semaphore_signal(barrier, inc=1, device_id=to, device_id_type=MESH)
    for to in (other_core, pair):
        pl.semaphore_signal(barrier, inc=1, device_id=to, device_id_type=MESH)

    kv[0, :, :width] = k_ref[...]
    kv[0, :, width:] = v_ref[...]
    for h in range(heads):
        at = pl.ds(pl.multiple_of(core * rows + h * blk, blk), blk)
        rows_q[at, :] = q_ref[:, h * width : (h + 1) * width]
        rows_do[at, :] = do_ref[:, h * width : (h + 1) * width]
    run_max[...] = jnp.full(run_max.shape, LOW, jnp.float32)
    run_sum[...] = jnp.zeros(run_sum.shape, jnp.float32)
    run_dot[...] = jnp.zeros(run_dot.shape, jnp.float32)

    pl.semaphore_wait(barrier, 2 * LINE + 2)

    def start_line(n, carry):
        line_copy(nearest(n)).start()
        return carry

    for c in core_copies():
        c.start()
    lax.fori_loop(0, AHEAD, start_line, 0)

    @pl.when(odd == 0)
    def _():
        pair_copy(0).start()

    def columns(base):
        def one(i, carry):
            at = pl.ds(pl.multiple_of(base + i * blk, blk), blk)
            cols_q[:, at] = rows_q[at, :].T
            cols_do[:, at] = rows_do[at, :].T
            return carry

        lax.fori_loop(0, heads, one, 0)

    columns(core * rows)
    for c in core_arrivals():
        c.wait_recv()
    columns((1 - core) * rows)

    def forward(slot, own):
        key_chip = (chip - slot + chips) % chips
        key_block = 2 * key_chip + core
        key_tag = doc_ref[key_block]
        key_tile = kv[slot, :, :width]
        value_tile = kv[slot, :, width:]
        keys_t[:, pl.ds(pl.multiple_of(slot * blk, blk), blk)] = key_tile.T

        def tile(i):
            at = pl.ds(i * COLS, COLS)
            query_half = i // tiles
            query_block = 2 * chip + query_half
            seen = (key_tag == doc_ref[query_block]) & (key_block <= query_block)
            s = jnp.dot(key_tile, cols_q[:, at], preferred_element_type=jnp.float32)
            dp = jnp.dot(value_tile, cols_do[:, at], preferred_element_type=jnp.float32)
            s = s * scale2
            if own:
                key_at = lax.broadcasted_iota(jnp.int32, (blk, COLS), 0)
                query_at = lax.broadcasted_iota(jnp.int32, (blk, COLS), 1) % blk
                s = jnp.where(
                    key_at - query_at <= (query_half - core) * blk, s, 2 * LOW
                )
            s3 = s.reshape(blk // 8, 8, COLS)
            dp3 = dp.reshape(blk // 8, 8, COLS)
            top = jnp.max(s3, axis=0)
            old = run_max[:, at]
            new = jnp.where(seen, jnp.maximum(old, top), old)
            used = jnp.where(seen, new, HIGH)
            w = jnp.exp2(s3 - used[None])
            factor = jnp.exp2(old - new)
            run_max[:, at] = new
            tile_max[slot, :, at] = new
            run_sum[:, at] = run_sum[:, at] * factor + jnp.sum(w, axis=0)
            run_dot[:, at] = run_dot[:, at] * factor + jnp.sum(w * dp3, axis=0)
            weights[slot, :, at] = w.reshape(blk, COLS)
            dprobs[slot, :, at] = dp

        for i in range(both):
            tile(i)

    forward(0, True)

    def gather_step(n, carry):
        @pl.when(n < LINE)
        def _():
            k = nearest(n)
            line_copy(k).wait_recv()

            @pl.when(n + AHEAD < LINE)
            def _():
                line_copy(nearest(n + AHEAD)).start()

            @pl.when((k < LINE) | (odd == 1))
            def _():
                pair_copy(k).start()

            forward(2 * k, False)

        @pl.when(n >= LAG)
        def _():
            k = nearest(n - LAG)
            b = jnp.where(odd == 1, k % LINE + 1, k)
            pair_arrival(b).wait_recv()
            forward(2 * b - 1, False)

        return carry

    lax.fori_loop(0, LINE + LAG, gather_step, 0)

    m8 = run_max[...]
    m1 = jnp.max(m8, axis=0, keepdims=True)
    f8 = jnp.exp2(m8 - m1)
    own_stats[0:1, :] = m1
    own_stats[1:2, :] = jnp.sum(run_sum[...] * f8, axis=0, keepdims=True)
    own_stats[2:3, :] = jnp.sum(run_dot[...] * f8, axis=0, keepdims=True)
    stats_copy = copy(
        own_stats, other_stats, core_send.at[2], core_recv.at[2], other_core
    )
    stats_copy.start()
    stats_copy.wait()
    ma, mb = own_stats[0:1, :], other_stats[0:1, :]
    m1 = jnp.maximum(ma, mb)
    fa, fb = jnp.exp2(ma - m1), jnp.exp2(mb - m1)
    total = own_stats[1:2, :] * fa + other_stats[1:2, :] * fb
    delta = (own_stats[2:3, :] * fa + other_stats[2:3, :] * fb) / total
    run_max[...] = jnp.broadcast_to(m1, run_max.shape)
    run_sum[...] = jnp.broadcast_to(1.0 / total, run_sum.shape)
    run_dot[...] = jnp.broadcast_to(delta, run_dot.shape)

    def backward(slot):
        def tile(i):
            at = pl.ds(i * COLS, COLS)
            factor = jnp.exp2(tile_max[slot, :, at] - run_max[:, at]) * run_sum[:, at]
            p3 = weights[slot, :, at].reshape(blk // 8, 8, COLS) * factor[None]
            dp3 = dprobs[slot, :, at].reshape(blk // 8, 8, COLS)
            ds3 = p3 * (dp3 - run_dot[:, at][None])
            low[:, at] = p3.reshape(blk, COLS).astype(jnp.bfloat16)
            dsc[pl.ds(pl.multiple_of(slot * blk, blk), blk), at] = ds3.reshape(
                blk, COLS
            ).astype(jnp.bfloat16)

        for i in range(both):
            tile(i)
        dv = jnp.dot(low[...], rows_do[...], preferred_element_type=jnp.float32)
        dk = jnp.dot(
            dsc[pl.ds(pl.multiple_of(slot * blk, blk), blk), :],
            rows_q[...],
            preferred_element_type=jnp.float32,
        )
        return dk * scale, dv

    @pl.when(odd == 0)
    def _():
        from_pair[LINE] = jnp.zeros(from_pair.shape[1:], jnp.bfloat16)

    @pl.when(odd == 1)
    def _():
        from_pair[0] = jnp.zeros(from_pair.shape[1:], jnp.bfloat16)

    def return_step(n, carry):
        @pl.when(n < LINE)
        def _():
            k = farthest(n)
            b = jnp.where(odd == 1, k % LINE + 1, k)
            dk, dv = backward(2 * b - 1)
            out_buf[2 * b - 1, :, :width] = dk.astype(jnp.bfloat16)
            out_buf[2 * b - 1, :, width:] = dv.astype(jnp.bfloat16)
            back_pair_copy(b).start()

        @pl.when(n >= BACK_LAG)
        def _():
            k = farthest(n - BACK_LAG)
            dk, dv = backward(2 * k)

            @pl.when((k < LINE) | (odd == 1))
            def _():
                back_pair_arrival(k).wait_recv()

            got = from_pair[k].astype(jnp.float32)
            out_buf[2 * k, :, :width] = (dk + got[:, :width]).astype(jnp.bfloat16)
            out_buf[2 * k, :, width:] = (dv + got[:, width:]).astype(jnp.bfloat16)
            back_line_copy(k).start()

        return carry

    lax.fori_loop(0, LINE + BACK_LAG, return_step, 0)

    dk, dv = backward(0)
    own_part[:, :width] = dk
    own_part[:, width:] = dv

    def query_tile(i):
        at = pl.ds(pl.multiple_of(i * COLS, COLS), COLS)
        part = jnp.dot(keys_t[...], dsc[:, at], preferred_element_type=jnp.float32)
        return (part * scale).T

    heads_tile = COLS // blk

    def far_rows(i, carry):
        part = query_tile((1 - core) * tiles + i).astype(jnp.bfloat16)
        for j in range(heads_tile):
            at = pl.ds(pl.multiple_of((i * heads_tile + j) * width, width), width)
            dq_send[:, at] = part[j * blk : (j + 1) * blk]
        return carry

    lax.fori_loop(0, tiles, far_rows, 0)
    dq_copy = copy(dq_send, dq_recv, core_send.at[3], core_recv.at[3], other_core)
    dq_copy.start()

    def near_rows(i, carry):
        part = query_tile(core * tiles + i)
        for j in range(heads_tile):
            at = pl.ds(pl.multiple_of((i * heads_tile + j) * width, width), width)
            near[:, at] = part[j * blk : (j + 1) * blk]
        return carry

    lax.fori_loop(0, tiles, near_rows, 0)
    dq_copy.wait()
    dq_ref[...] = (near[...] + dq_recv[...].astype(jnp.float32)).astype(jnp.bfloat16)

    @pl.when(odd == 0)
    def _():
        back_pair_arrival(0).wait_recv()

    own_part[...] += from_pair[0].astype(jnp.float32)

    def add_line(n, carry):
        k = farthest(n)
        back_line_copy(k).wait_recv()
        own_part[...] += from_line[k].astype(jnp.float32)
        return carry

    lax.fori_loop(0, LINE, add_line, 0)
    dk_ref[...] = own_part[:, :width].astype(jnp.bfloat16)
    dv_ref[...] = own_part[:, width:].astype(jnp.bfloat16)

    def finish(n, carry):
        k = n + 1
        line_copy(k).wait_send()
        back_line_copy(k).wait_send()
        pair_copy(n + odd).wait_send()
        back_pair_copy(k).wait_send()
        return carry

    lax.fori_loop(0, LINE, finish, 0)
    for c in core_copies():
        c.wait_send()


def solution(mesh):
    inner_count = mesh.shape["inner"]
    devices = inner_count * mesh.shape["outer"]

    def shards(queries, key_rows, value_rows, grad_output, doc_blocks):
        blk, width = key_rows.shape
        heads = queries.shape[1] // width
        rows = heads * blk
        bf16, f32 = jnp.bfloat16, jnp.float32
        vmem = pl.BlockSpec(memory_space=pltpu.VMEM)
        dma = pltpu.SemaphoreType.DMA
        return pl.pallas_call(
            functools.partial(kernel, inner_count, devices // 2, blk, width, heads),
            name="attention_backward",
            out_shape=(
                jax.ShapeDtypeStruct(queries.shape, bf16),
                jax.ShapeDtypeStruct(key_rows.shape, bf16),
                jax.ShapeDtypeStruct(value_rows.shape, bf16),
            ),
            in_specs=[vmem] * 4 + [pl.BlockSpec(memory_space=pltpu.SMEM)],
            out_specs=(vmem, vmem, vmem),
            scratch_shapes=[
                pltpu.VMEM((SLOTS, blk, 2 * width), bf16),
                pltpu.VMEM((width, SLOTS * blk), bf16),
                pltpu.VMEM((2 * rows, width), bf16),
                pltpu.VMEM((2 * rows, width), bf16),
                pltpu.VMEM((width, 2 * rows), bf16),
                pltpu.VMEM((width, 2 * rows), bf16),
                pltpu.VMEM((SLOTS, blk, 2 * rows), f32),
                pltpu.VMEM((SLOTS, blk, 2 * rows), f32),
                pltpu.VMEM((SLOTS, 8, 2 * rows), f32),
                pltpu.VMEM((8, 2 * rows), f32),
                pltpu.VMEM((8, 2 * rows), f32),
                pltpu.VMEM((8, 2 * rows), f32),
                pltpu.VMEM((3, 2 * rows), f32),
                pltpu.VMEM((3, 2 * rows), f32),
                pltpu.VMEM((blk, 2 * rows), bf16),
                pltpu.VMEM((SLOTS * blk, 2 * rows), bf16),
                pltpu.VMEM((SLOTS, blk, 2 * width), bf16),
                pltpu.VMEM((LINE + 1, blk, 2 * width), bf16),
                pltpu.VMEM((LINE + 1, blk, 2 * width), bf16),
                pltpu.VMEM((blk, 2 * width), f32),
                pltpu.VMEM((blk, heads * width), f32),
                pltpu.VMEM((blk, heads * width), bf16),
                pltpu.VMEM((blk, heads * width), bf16),
                dma((LINE + 1,)),
                dma((LINE + 1,)),
                dma((LINE + 1,)),
                dma((LINE + 1,)),
                dma((LINE + 1,)),
                dma((LINE + 1,)),
                dma((LINE + 1,)),
                dma((LINE + 1,)),
                dma((4,)),
                dma((4,)),
            ],
            compiler_params=pltpu.CompilerParams(
                collective_id=0, has_side_effects=True, vmem_limit_bytes=60 << 20
            ),
        )(queries, key_rows, value_rows, grad_output, doc_blocks)

    rows = P(("outer", "inner"), None)
    return jax.shard_map(
        shards,
        mesh=mesh,
        in_specs=(rows, rows, rows, rows, P()),
        out_specs=(rows, rows, rows),
        check_vma=False,
    )
```

```python
import functools
import math

import jax
import jax.numpy as jnp
from jax import lax
from jax.experimental import pallas as pl
from jax.experimental.pallas import tpu as pltpu
from jax.sharding import PartitionSpec as P

MESH = pl.DeviceIdType.MESH
WINDOW = 16
LINE = WINDOW // 2
SLOTS = WINDOW + 1
COLS = 256
ROUTE = {
    1: (-1, 0),
    2: (-2, 0),
    8: (-8, 0),
    3: (-1, 2),
    4: (-2, 2),
    7: (1, 8),
    6: (2, 8),
    5: (3, 8),
}
REACH = (1, 2, 3, 8)
HUBS = (8, 2, 1)
BACK = (("other", 4), ("other", 3), ("other", 6), ("other", 5), ("other", 7))
BACK += (("other", 2), ("line", 4), ("line", 3), ("line", 6), ("line", 5))
BACK += (("line", 7), ("other", 8), ("other", 1), ("line", 8), ("line", 2))
BACK += (("line", 1), ("own", 0))
LOW = -1e30
HIGH = 3e38


def choose(n, values):
    out = values[0]
    for j in range(1, len(values)):
        out = jnp.where(n == j, values[j], out)
    return out


def at_step(n, actions):
    for j, one in actions.items():
        pl.when(n == j)(one)


def kernel(
    inner_count,
    chips,
    blk,
    width,
    heads,
    q_ref,
    k_ref,
    v_ref,
    do_ref,
    doc_ref,
    dq_ref,
    dk_ref,
    dv_ref,
    kv,
    keys_t,
    rows_q,
    rows_do,
    cols_q,
    cols_do,
    weights,
    dprobs,
    tile_max,
    run_max,
    run_sum,
    run_dot,
    own_stats,
    other_stats,
    low,
    dsc,
    out_buf,
    from_pair,
    from_line,
    parts,
    near,
    dq_send,
    dq_recv,
    line_send,
    line_recv,
    pair_send,
    pair_recv,
    back_line_send,
    back_line_recv,
    back_pair_send,
    back_pair_recv,
    core_send,
    core_recv,
    load_sem,
):
    rows = heads * blk
    tiles = rows // COLS
    both = 2 * tiles
    scale = width ** (-0.5)
    scale2 = scale * math.log2(math.e)
    per_group = inner_count // 2

    outer = lax.axis_index("outer")
    inner = lax.axis_index("inner")
    core = inner % 2
    chip = outer * per_group + inner // 2
    odd = chip % 2

    def device(chip_at, core_at):
        return {
            "outer": chip_at // per_group,
            "inner": (chip_at % per_group) * 2 + core_at,
        }

    def unit(k):
        return device((chip + 2 * k + chips) % chips, core)

    other_core = device(chip, 1 - core)
    pair = device(chip + 1 - 2 * odd, core)

    def copy(src, dst, send, recv, to):
        return pltpu.make_async_remote_copy(
            src_ref=src,
            dst_ref=dst,
            send_sem=send,
            recv_sem=recv,
            device_id=to,
            device_id_type=MESH,
        )

    def other(k):
        return 2 * k - 1 + 2 * odd if k < LINE else 2 * LINE - 1 - (2 * LINE - 2) * odd

    def line_copy(k):
        step, held = ROUTE[k]
        return copy(
            kv.at[2 * held], kv.at[2 * k], line_send.at[k], line_recv.at[k], unit(-step)
        )

    def pair_copy(k):
        src = 2 * k if k < LINE else 2 * LINE * odd
        dst = 2 * k + 1 - 2 * odd if k < LINE else 1 + (2 * LINE - 2) * odd
        return copy(
            kv.at[src], kv.at[dst], pair_send.at[k], pair_recv.at[k], pair
        )

    def pair_arrival(k):
        return copy(
            kv.at[0], kv.at[other(k)], pair_send.at[k], pair_recv.at[k], pair
        )

    def back_pair_copy(k):
        return copy(
            out_buf.at[other(k)], from_pair.at[k], back_pair_send.at[k],
            back_pair_recv.at[k], pair,
        )

    def back_line_copy(k):
        step, held = ROUTE[k]
        return copy(
            out_buf.at[2 * k], from_line.at[k], back_line_send.at[k],
            back_line_recv.at[k], unit(step),
        )

    def core_copies():
        own = pl.ds(pl.multiple_of(core * rows, rows), rows)
        return (
            copy(
                rows_q.at[own], rows_q.at[own], core_send.at[0], core_recv.at[0],
                other_core,
            ),
            copy(
                rows_do.at[own], rows_do.at[own], core_send.at[1], core_recv.at[1],
                other_core,
            ),
        )

    def core_arrivals():
        own = pl.ds(pl.multiple_of((1 - core) * rows, rows), rows)
        return (
            copy(
                rows_q.at[own], rows_q.at[own], core_send.at[0], core_recv.at[0],
                other_core,
            ),
            copy(
                rows_do.at[own], rows_do.at[own], core_send.at[1], core_recv.at[1],
                other_core,
            ),
        )

    barrier = pltpu.get_barrier_semaphore()
    for k in REACH:
        for to in (unit(k), unit(-k)):
            pl.semaphore_signal(barrier, inc=1, device_id=to, device_id_type=MESH)
    for to in (other_core, pair):
        pl.semaphore_signal(barrier, inc=1, device_id=to, device_id_type=MESH)

    loads = [
        pltpu.make_async_copy(k_ref, kv.at[0, :, pl.ds(0, width)], load_sem.at[0]),
        pltpu.make_async_copy(v_ref, kv.at[0, :, pl.ds(width, width)], load_sem.at[1]),
    ]
    for h in range(heads):
        at = pl.ds(pl.multiple_of(core * rows + h * blk, blk), blk)
        of = pl.ds(h * width, width)
        for j, (src, dst) in enumerate(((q_ref, rows_q), (do_ref, rows_do))):
            loads.append(
                pltpu.make_async_copy(
                    src.at[:, of], dst.at[at], load_sem.at[2 + 2 * h + j]
                )
            )
    for c in loads:
        c.start()
    run_max[...] = jnp.full(run_max.shape, LOW, jnp.float32)
    run_sum[...] = jnp.zeros(run_sum.shape, jnp.float32)
    run_dot[...] = jnp.zeros(run_dot.shape, jnp.float32)

    pl.semaphore_wait(barrier, 2 * len(REACH) + 2)

    def on_even(run):
        pl.when(odd == 0)(run)

    for c in loads[:2]:
        c.wait()
    for k in (2, 8, 1):
        line_copy(k).start()
    on_even(lambda: pair_copy(LINE).start())
    for c in loads[2:]:
        c.wait()
    for c in core_copies():
        c.start()

    def columns(base):
        def one(i, carry):
            at = pl.ds(pl.multiple_of(base + i * blk, blk), blk)
            cols_q[:, at] = rows_q[at, :].T
            cols_do[:, at] = rows_do[at, :].T
            return carry

        lax.fori_loop(0, heads, one, 0)

    columns(core * rows)
    for c in core_arrivals():
        c.wait_recv()
    columns((1 - core) * rows)

    def pass_on(k):
        line_copy(k).wait_recv()
        for far, (step, held) in ROUTE.items():
            if held == k:
                line_copy(far).start()
        if k < LINE:
            pair_copy(k).start()
        else:
            pl.when(odd == 1)(lambda: pair_copy(k).start())

    for k in (8, 2, 1):
        pass_on(k)

    def forward(slot, own):
        key_chip = (chip - slot + chips) % chips
        key_block = 2 * key_chip + core
        key_tag = doc_ref[key_block]
        key_tile = kv[slot, :, :width]
        value_tile = kv[slot, :, width:]
        keys_t[:, pl.ds(pl.multiple_of(slot * blk, blk), blk)] = key_tile.T

        def tile(i):
            at = pl.ds(i * COLS, COLS)
            query_half = i // tiles
            query_block = 2 * chip + query_half
            seen = (key_tag == doc_ref[query_block]) & (key_block <= query_block)
            s = jnp.dot(key_tile, cols_q[:, at], preferred_element_type=jnp.float32)
            dp = jnp.dot(value_tile, cols_do[:, at], preferred_element_type=jnp.float32)
            s = s * scale2
            if own:
                key_at = lax.broadcasted_iota(jnp.int32, (blk, COLS), 0)
                query_at = lax.broadcasted_iota(jnp.int32, (blk, COLS), 1) % blk
                s = jnp.where(
                    key_at - query_at <= (query_half - core) * blk, s, 2 * LOW
                )
            s3 = s.reshape(blk // 8, 8, COLS)
            dp3 = dp.reshape(blk // 8, 8, COLS)
            top = jnp.max(s3, axis=0)
            old = run_max[:, at]
            new = jnp.where(seen, jnp.maximum(old, top), old)
            used = jnp.where(seen, new, HIGH)
            w = jnp.exp2(s3 - used[None])
            factor = jnp.exp2(old - new)
            run_max[:, at] = new
            tile_max[slot, :, at] = new
            run_sum[:, at] = run_sum[:, at] * factor + jnp.sum(w, axis=0)
            run_dot[:, at] = run_dot[:, at] * factor + jnp.sum(w * dp3, axis=0)
            weights[slot, :, at] = w.reshape(blk, COLS)
            dprobs[slot, :, at] = dp

        for i in range(both):
            tile(i)

    forward(0, True)

    def take(*ks):
        def run():
            for k in ks:
                pass_on(k)

        return run

    def arrived(k):
        return lambda: pair_arrival(k).wait_recv()

    order = (16, 4, 2, 14, 6, 12, 8, 10, other(8), other(1), other(2), other(7))
    order += (other(3), other(6), other(4), other(5))
    before = {3: take(7), 4: take(3), 5: take(6, 4, 5)}
    for j, k in ((8, 8), (9, 1), (10, 2), (11, 7), (12, 3), (13, 6), (14, 4), (15, 5)):
        before[j] = arrived(k)

    def gather_step(n, carry):
        at_step(n, before)
        forward(choose(n, order), False)
        return carry

    lax.fori_loop(0, len(order), gather_step, 0)

    m8 = run_max[...]
    m1 = jnp.max(m8, axis=0, keepdims=True)
    f8 = jnp.exp2(m8 - m1)
    own_stats[0:1, :] = m1
    own_stats[1:2, :] = jnp.sum(run_sum[...] * f8, axis=0, keepdims=True)
    own_stats[2:3, :] = jnp.sum(run_dot[...] * f8, axis=0, keepdims=True)
    stats_copy = copy(
        own_stats, other_stats, core_send.at[2], core_recv.at[2], other_core
    )
    stats_copy.start()
    stats_copy.wait()
    ma, mb = own_stats[0:1, :], other_stats[0:1, :]
    m1 = jnp.maximum(ma, mb)
    fa, fb = jnp.exp2(ma - m1), jnp.exp2(mb - m1)
    total = own_stats[1:2, :] * fa + other_stats[1:2, :] * fb
    delta = (own_stats[2:3, :] * fa + other_stats[2:3, :] * fb) / total
    run_max[...] = jnp.broadcast_to(m1, run_max.shape)
    run_sum[...] = jnp.broadcast_to(1.0 / total, run_sum.shape)
    run_dot[...] = jnp.broadcast_to(delta, run_dot.shape)

    def backward(slot):
        def tile(i):
            at = pl.ds(i * COLS, COLS)
            factor = jnp.exp2(tile_max[slot, :, at] - run_max[:, at]) * run_sum[:, at]
            p3 = weights[slot, :, at].reshape(blk // 8, 8, COLS) * factor[None]
            dp3 = dprobs[slot, :, at].reshape(blk // 8, 8, COLS)
            ds3 = p3 * (dp3 - run_dot[:, at][None])
            low[:, at] = p3.reshape(blk, COLS).astype(jnp.bfloat16)
            dsc[pl.ds(pl.multiple_of(slot * blk, blk), blk), at] = ds3.reshape(
                blk, COLS
            ).astype(jnp.bfloat16)

        for i in range(both):
            tile(i)
        dv = jnp.dot(low[...], rows_do[...], preferred_element_type=jnp.float32)
        dk = jnp.dot(
            dsc[pl.ds(pl.multiple_of(slot * blk, blk), blk), :],
            rows_q[...],
            preferred_element_type=jnp.float32,
        )
        return dk * scale, dv

    from_pair[0] = jnp.zeros(from_pair.shape[1:], jnp.bfloat16)

    def back_arrived(k):
        return lambda: back_pair_copy(k).wait_recv()

    def starts(copy_of, k):
        return lambda: copy_of(k).start()

    back_order = []
    back_add = []
    back_part = []
    back_before = {}
    back_after = {}
    for j, (kind, k) in enumerate(BACK):
        back_order.append(other(k) if kind == "other" else 2 * k)
        back_add.append(0)
        back_part.append(len(HUBS) + 1)
        if kind == "other":
            back_after[j] = starts(back_pair_copy, k)
        elif kind == "own":
            back_part[j] = 0
        elif k in HUBS:
            back_part[j] = 1 + HUBS.index(k)
        else:
            back_add[j] = k
            back_before[j] = back_arrived(k)
            back_after[j] = starts(back_line_copy, k)

    def return_step(n, carry):
        slot = choose(n, back_order)
        dk, dv = backward(slot)
        at_step(n, back_before)
        got = from_pair[choose(n, back_add)].astype(jnp.float32)
        part = choose(n, back_part)
        dk = dk + got[:, :width]
        dv = dv + got[:, width:]
        parts[part, :, :width] = dk
        parts[part, :, width:] = dv
        out_buf[slot, :, :width] = dk.astype(jnp.bfloat16)
        out_buf[slot, :, width:] = dv.astype(jnp.bfloat16)
        at_step(n, back_after)
        return carry

    lax.fori_loop(0, len(BACK), return_step, 0)

    def finish_hub(k):
        at = 1 + HUBS.index(k)

        def add_pair():
            back_pair_copy(k).wait_recv()
            parts[at] += from_pair[k].astype(jnp.float32)

        if k < LINE:
            add_pair()
        else:
            pl.when(odd == 1)(add_pair)
        total = parts[at]
        for m, (step, held) in ROUTE.items():
            if held == k:
                back_line_copy(m).wait_recv()
                total = total + from_line[m].astype(jnp.float32)
        out_buf[2 * k] = total.astype(jnp.bfloat16)
        back_line_copy(k).start()

    def query_tile(i):
        at = pl.ds(pl.multiple_of(i * COLS, COLS), COLS)
        part = jnp.dot(keys_t[...], dsc[:, at], preferred_element_type=jnp.float32)
        return (part * scale).T

    heads_tile = COLS // blk

    def far_rows(i, carry):
        part = query_tile((1 - core) * tiles + i).astype(jnp.bfloat16)
        for j in range(heads_tile):
            at = pl.ds(pl.multiple_of((i * heads_tile + j) * width, width), width)
            dq_send[:, at] = part[j * blk : (j + 1) * blk]
        return carry

    lax.fori_loop(0, tiles, far_rows, 0)
    dq_copy = copy(dq_send, dq_recv, core_send.at[3], core_recv.at[3], other_core)
    dq_copy.start()
    for k in HUBS:
        finish_hub(k)

    def near_rows(i, carry):
        part = query_tile(core * tiles + i)
        for j in range(heads_tile):
            at = pl.ds(pl.multiple_of((i * heads_tile + j) * width, width), width)
            near[:, at] = part[j * blk : (j + 1) * blk]
        return carry

    lax.fori_loop(0, tiles, near_rows, 0)
    dq_copy.wait()
    dq_ref[...] = (near[...] + dq_recv[...].astype(jnp.float32)).astype(jnp.bfloat16)

    @pl.when(odd == 0)
    def _():
        back_pair_copy(LINE).wait_recv()
        parts[0] += from_pair[LINE].astype(jnp.float32)

    total = parts[0]
    for k in (1, 8, 2):
        back_line_copy(k).wait_recv()
        total = total + from_line[k].astype(jnp.float32)
    dk_ref[...] = total[:, :width].astype(jnp.bfloat16)
    dv_ref[...] = total[:, width:].astype(jnp.bfloat16)

    for k in range(1, LINE + 1):
        line_copy(k).wait_send()
        back_line_copy(k).wait_send()
        pair_copy(k).wait_send()
        back_pair_copy(k).wait_send()
    for c in core_copies():
        c.wait_send()


def hand_out(dq_ref, dk_ref, dv_ref, dq_out, dk_out, dv_out):
    dq_out[...] = dq_ref[...]
    dk_out[...] = dk_ref[...]
    dv_out[...] = dv_ref[...]


def solution(mesh):
    inner_count = mesh.shape["inner"]
    devices = inner_count * mesh.shape["outer"]

    def shards(queries, key_rows, value_rows, grad_output, doc_blocks):
        blk, width = key_rows.shape
        heads = queries.shape[1] // width
        rows = heads * blk
        bf16, f32 = jnp.bfloat16, jnp.float32
        vmem = pl.BlockSpec(memory_space=pltpu.VMEM)
        dma = pltpu.SemaphoreType.DMA
        grads = pl.pallas_call(
            functools.partial(kernel, inner_count, devices // 2, blk, width, heads),
            name="attention_backward",
            out_shape=(
                jax.ShapeDtypeStruct(queries.shape, bf16),
                jax.ShapeDtypeStruct(key_rows.shape, bf16),
                jax.ShapeDtypeStruct(value_rows.shape, bf16),
            ),
            in_specs=[pl.BlockSpec(memory_space=pl.ANY)] * 4 + [pl.BlockSpec(memory_space=pltpu.SMEM)],
            out_specs=(vmem, vmem, vmem),
            scratch_shapes=[
                pltpu.VMEM((SLOTS, blk, 2 * width), bf16),
                pltpu.VMEM((width, SLOTS * blk), bf16),
                pltpu.VMEM((2 * rows, width), bf16),
                pltpu.VMEM((2 * rows, width), bf16),
                pltpu.VMEM((width, 2 * rows), bf16),
                pltpu.VMEM((width, 2 * rows), bf16),
                pltpu.VMEM((SLOTS, blk, 2 * rows), f32),
                pltpu.VMEM((SLOTS, blk, 2 * rows), f32),
                pltpu.VMEM((SLOTS, 8, 2 * rows), f32),
                pltpu.VMEM((8, 2 * rows), f32),
                pltpu.VMEM((8, 2 * rows), f32),
                pltpu.VMEM((8, 2 * rows), f32),
                pltpu.VMEM((3, 2 * rows), f32),
                pltpu.VMEM((3, 2 * rows), f32),
                pltpu.VMEM((blk, 2 * rows), bf16),
                pltpu.VMEM((SLOTS * blk, 2 * rows), bf16),
                pltpu.VMEM((SLOTS, blk, 2 * width), bf16),
                pltpu.VMEM((LINE + 1, blk, 2 * width), bf16),
                pltpu.VMEM((LINE + 1, blk, 2 * width), bf16),
                pltpu.VMEM((len(HUBS) + 2, blk, 2 * width), f32),
                pltpu.VMEM((blk, heads * width), f32),
                pltpu.VMEM((blk, heads * width), bf16),
                pltpu.VMEM((blk, heads * width), bf16),
                dma((LINE + 1,)),
                dma((LINE + 1,)),
                dma((LINE + 1,)),
                dma((LINE + 1,)),
                dma((LINE + 1,)),
                dma((LINE + 1,)),
                dma((LINE + 1,)),
                dma((LINE + 1,)),
                dma((4,)),
                dma((4,)),
                dma((2 + 2 * heads,)),
            ],
            compiler_params=pltpu.CompilerParams(
                collective_id=0, has_side_effects=True, vmem_limit_bytes=56 << 20
            ),
        )(queries, key_rows, value_rows, grad_output, doc_blocks)
        return pl.pallas_call(
            hand_out,
            name="hand_out",
            out_shape=[jax.ShapeDtypeStruct(x.shape, x.dtype) for x in grads],
            in_specs=[vmem] * 3,
            out_specs=[vmem] * 3,
        )(*grads)

    rows = P(("outer", "inner"), None)
    return jax.shard_map(
        shards,
        mesh=mesh,
        in_specs=(rows, rows, rows, rows, P()),
        out_specs=(rows, rows, rows),
        check_vma=False,
    )
```

```python
import functools
import math

import jax
import jax.numpy as jnp
from jax import lax
from jax.experimental import pallas as pl
from jax.experimental.pallas import tpu as pltpu
from jax.sharding import PartitionSpec as P

MESH = pl.DeviceIdType.MESH
WINDOW = 16
LINE = WINDOW // 2
SLOTS = WINDOW + 1
COLS = 256
ROUTE = {
    1: (-1, 0),
    2: (-2, 0),
    8: (-8, 0),
    6: (-6, 0),
    3: (-1, 2),
    4: (-2, 2),
    7: (1, 8),
    5: (1, 6),
}
REACH = (1, 2, 6, 8)
HUBS = (6, 8, 2, 1)
BACK = (("other", 4), ("other", 5), ("other", 3), ("other", 7), ("other", 6))
BACK += (("other", 2), ("line", 4), ("line", 5), ("line", 3), ("line", 7))
BACK += (("other", 8), ("other", 1), ("line", 6), ("line", 2), ("line", 8))
BACK += (("line", 1), ("own", 0))
LOW = -1e30
HIGH = 3e38


def choose(n, values):
    out = values[0]
    for j in range(1, len(values)):
        out = jnp.where(n == j, values[j], out)
    return out


def at_step(n, actions):
    for j, one in actions.items():
        pl.when(n == j)(one)


def kernel(
    inner_count,
    chips,
    blk,
    width,
    heads,
    q_ref,
    k_ref,
    v_ref,
    do_ref,
    doc_ref,
    dq_ref,
    dk_ref,
    dv_ref,
    kv,
    keys_t,
    rows_q,
    rows_do,
    cols_q,
    cols_do,
    weights,
    dprobs,
    tile_max,
    run_max,
    run_sum,
    run_dot,
    own_stats,
    other_stats,
    low,
    dsc,
    out_buf,
    from_pair,
    from_line,
    parts,
    near,
    dq_send,
    dq_recv,
    line_send,
    line_recv,
    pair_send,
    pair_recv,
    back_line_send,
    back_line_recv,
    back_pair_send,
    back_pair_recv,
    core_send,
    core_recv,
    load_sem,
):
    rows = heads * blk
    tiles = rows // COLS
    both = 2 * tiles
    scale = width ** (-0.5)
    scale2 = scale * math.log2(math.e)
    per_group = inner_count // 2

    outer = lax.axis_index("outer")
    inner = lax.axis_index("inner")
    core = inner % 2
    chip = outer * per_group + inner // 2
    odd = chip % 2

    def device(chip_at, core_at):
        return {
            "outer": chip_at // per_group,
            "inner": (chip_at % per_group) * 2 + core_at,
        }

    def unit(k):
        return device((chip + 2 * k + chips) % chips, core)

    other_core = device(chip, 1 - core)
    pair = device(chip + 1 - 2 * odd, core)

    def copy(src, dst, send, recv, to):
        return pltpu.make_async_remote_copy(
            src_ref=src,
            dst_ref=dst,
            send_sem=send,
            recv_sem=recv,
            device_id=to,
            device_id_type=MESH,
        )

    def other(k):
        return 2 * k - 1 + 2 * odd if k < LINE else 2 * LINE - 1 - (2 * LINE - 2) * odd

    def line_copy(k):
        step, held = ROUTE[k]
        return copy(
            kv.at[2 * held], kv.at[2 * k], line_send.at[k], line_recv.at[k], unit(-step)
        )

    def pair_copy(k):
        src = 2 * k if k < LINE else 2 * LINE * odd
        dst = 2 * k + 1 - 2 * odd if k < LINE else 1 + (2 * LINE - 2) * odd
        return copy(
            kv.at[src], kv.at[dst], pair_send.at[k], pair_recv.at[k], pair
        )

    def pair_arrival(k):
        return copy(
            kv.at[0], kv.at[other(k)], pair_send.at[k], pair_recv.at[k], pair
        )

    def back_pair_copy(k):
        return copy(
            out_buf.at[other(k)], from_pair.at[k], back_pair_send.at[k],
            back_pair_recv.at[k], pair,
        )

    def back_line_copy(k):
        step, held = ROUTE[k]
        return copy(
            out_buf.at[2 * k], from_line.at[k], back_line_send.at[k],
            back_line_recv.at[k], unit(step),
        )

    def core_copies():
        own = pl.ds(pl.multiple_of(core * rows, rows), rows)
        return (
            copy(
                rows_q.at[own], rows_q.at[own], core_send.at[0], core_recv.at[0],
                other_core,
            ),
            copy(
                rows_do.at[own], rows_do.at[own], core_send.at[1], core_recv.at[1],
                other_core,
            ),
        )

    def core_arrivals():
        own = pl.ds(pl.multiple_of((1 - core) * rows, rows), rows)
        return (
            copy(
                rows_q.at[own], rows_q.at[own], core_send.at[0], core_recv.at[0],
                other_core,
            ),
            copy(
                rows_do.at[own], rows_do.at[own], core_send.at[1], core_recv.at[1],
                other_core,
            ),
        )

    barrier = pltpu.get_barrier_semaphore()
    for k in REACH:
        for to in (unit(k), unit(-k)):
            pl.semaphore_signal(barrier, inc=1, device_id=to, device_id_type=MESH)
    for to in (other_core, pair):
        pl.semaphore_signal(barrier, inc=1, device_id=to, device_id_type=MESH)

    loads = [
        pltpu.make_async_copy(k_ref, kv.at[0, :, pl.ds(0, width)], load_sem.at[0]),
        pltpu.make_async_copy(v_ref, kv.at[0, :, pl.ds(width, width)], load_sem.at[1]),
    ]
    for h in range(heads):
        at = pl.ds(pl.multiple_of(core * rows + h * blk, blk), blk)
        of = pl.ds(h * width, width)
        for j, (src, dst) in enumerate(((q_ref, rows_q), (do_ref, rows_do))):
            loads.append(
                pltpu.make_async_copy(
                    src.at[:, of], dst.at[at], load_sem.at[2 + 2 * h + j]
                )
            )
    for c in loads:
        c.start()
    run_max[...] = jnp.full(run_max.shape, LOW, jnp.float32)
    run_sum[...] = jnp.zeros(run_sum.shape, jnp.float32)
    run_dot[...] = jnp.zeros(run_dot.shape, jnp.float32)

    pl.semaphore_wait(barrier, 2 * len(REACH) + 2)

    def on_even(run):
        pl.when(odd == 0)(run)

    for c in loads[:2]:
        c.wait()
    for k in (6, 2, 8, 1):
        line_copy(k).start()
    on_even(lambda: pair_copy(LINE).start())
    for c in loads[2:]:
        c.wait()
    for c in core_copies():
        c.start()

    def columns(base):
        def one(i, carry):
            at = pl.ds(pl.multiple_of(base + i * blk, blk), blk)
            cols_q[:, at] = rows_q[at, :].T
            cols_do[:, at] = rows_do[at, :].T
            return carry

        lax.fori_loop(0, heads, one, 0)

    columns(core * rows)
    for c in core_arrivals():
        c.wait_recv()
    columns((1 - core) * rows)

    def pass_on(k):
        line_copy(k).wait_recv()
        for far, (step, held) in ROUTE.items():
            if held == k:
                line_copy(far).start()
        if k < LINE:
            pair_copy(k).start()
        else:
            pl.when(odd == 1)(lambda: pair_copy(k).start())

    for k in (8, 2, 1):
        pass_on(k)

    def forward(slot, own):
        key_chip = (chip - slot + chips) % chips
        key_block = 2 * key_chip + core
        key_tag = doc_ref[key_block]
        key_tile = kv[slot, :, :width]
        value_tile = kv[slot, :, width:]
        keys_t[:, pl.ds(pl.multiple_of(slot * blk, blk), blk)] = key_tile.T

        def tile(i):
            at = pl.ds(i * COLS, COLS)
            query_half = i // tiles
            query_block = 2 * chip + query_half
            seen = (key_tag == doc_ref[query_block]) & (key_block <= query_block)
            s = jnp.dot(key_tile, cols_q[:, at], preferred_element_type=jnp.float32)
            dp = jnp.dot(value_tile, cols_do[:, at], preferred_element_type=jnp.float32)
            s = s * scale2
            if own:
                key_at = lax.broadcasted_iota(jnp.int32, (blk, COLS), 0)
                query_at = lax.broadcasted_iota(jnp.int32, (blk, COLS), 1) % blk
                s = jnp.where(
                    key_at - query_at <= (query_half - core) * blk, s, 2 * LOW
                )
            s3 = s.reshape(blk // 8, 8, COLS)
            dp3 = dp.reshape(blk // 8, 8, COLS)
            top = jnp.max(s3, axis=0)
            old = run_max[:, at]
            new = jnp.where(seen, jnp.maximum(old, top), old)
            used = jnp.where(seen, new, HIGH)
            w = jnp.exp2(s3 - used[None])
            factor = jnp.exp2(old - new)
            run_max[:, at] = new
            tile_max[slot, :, at] = new
            run_sum[:, at] = run_sum[:, at] * factor + jnp.sum(w, axis=0)
            run_dot[:, at] = run_dot[:, at] * factor + jnp.sum(w * dp3, axis=0)
            weights[slot, :, at] = w.reshape(blk, COLS)
            dprobs[slot, :, at] = dp

        for i in range(both):
            tile(i)

    forward(0, True)

    def take(*ks):
        def run():
            for k in ks:
                pass_on(k)

        return run

    def arrived(k):
        return lambda: pair_arrival(k).wait_recv()

    order = (16, 4, 12, 2, 14, 6, 10, 8, other(8), other(2), other(1), other(6))
    order += (other(7), other(3), other(5), other(4))
    before = {2: take(6), 4: take(7), 5: take(3), 6: take(5, 4)}
    for j, k in ((8, 8), (9, 2), (10, 1), (11, 6), (12, 7), (13, 3), (14, 5), (15, 4)):
        before[j] = arrived(k)

    def gather_step(n, carry):
        at_step(n, before)
        forward(choose(n, order), False)
        return carry

    lax.fori_loop(0, len(order), gather_step, 0)

    m8 = run_max[...]
    m1 = jnp.max(m8, axis=0, keepdims=True)
    f8 = jnp.exp2(m8 - m1)
    own_stats[0:1, :] = m1
    own_stats[1:2, :] = jnp.sum(run_sum[...] * f8, axis=0, keepdims=True)
    own_stats[2:3, :] = jnp.sum(run_dot[...] * f8, axis=0, keepdims=True)
    stats_copy = copy(
        own_stats, other_stats, core_send.at[2], core_recv.at[2], other_core
    )
    stats_copy.start()
    stats_copy.wait()
    ma, mb = own_stats[0:1, :], other_stats[0:1, :]
    m1 = jnp.maximum(ma, mb)
    fa, fb = jnp.exp2(ma - m1), jnp.exp2(mb - m1)
    total = own_stats[1:2, :] * fa + other_stats[1:2, :] * fb
    delta = (own_stats[2:3, :] * fa + other_stats[2:3, :] * fb) / total
    run_max[...] = jnp.broadcast_to(m1, run_max.shape)
    run_sum[...] = jnp.broadcast_to(1.0 / total, run_sum.shape)
    run_dot[...] = jnp.broadcast_to(delta, run_dot.shape)

    def backward(slot):
        def tile(i):
            at = pl.ds(i * COLS, COLS)
            factor = jnp.exp2(tile_max[slot, :, at] - run_max[:, at]) * run_sum[:, at]
            p3 = weights[slot, :, at].reshape(blk // 8, 8, COLS) * factor[None]
            dp3 = dprobs[slot, :, at].reshape(blk // 8, 8, COLS)
            ds3 = p3 * (dp3 - run_dot[:, at][None])
            low[:, at] = p3.reshape(blk, COLS).astype(jnp.bfloat16)
            dsc[pl.ds(pl.multiple_of(slot * blk, blk), blk), at] = ds3.reshape(
                blk, COLS
            ).astype(jnp.bfloat16)

        for i in range(both):
            tile(i)
        dv = jnp.dot(low[...], rows_do[...], preferred_element_type=jnp.float32)
        dk = jnp.dot(
            dsc[pl.ds(pl.multiple_of(slot * blk, blk), blk), :],
            rows_q[...],
            preferred_element_type=jnp.float32,
        )
        return dk * scale, dv

    from_pair[0] = jnp.zeros(from_pair.shape[1:], jnp.bfloat16)

    def back_arrived(k):
        return lambda: back_pair_copy(k).wait_recv()

    def starts(copy_of, k):
        return lambda: copy_of(k).start()

    back_order = []
    back_add = []
    back_part = []
    back_before = {}
    back_after = {}
    for j, (kind, k) in enumerate(BACK):
        back_order.append(other(k) if kind == "other" else 2 * k)
        back_add.append(0)
        back_part.append(len(HUBS) + 1)
        if kind == "other":
            back_after[j] = starts(back_pair_copy, k)
        elif kind == "own":
            back_part[j] = 0
        elif k in HUBS:
            back_part[j] = 1 + HUBS.index(k)
        else:
            back_add[j] = k
            back_before[j] = back_arrived(k)
            back_after[j] = starts(back_line_copy, k)

    def return_step(n, carry):
        slot = choose(n, back_order)
        dk, dv = backward(slot)
        at_step(n, back_before)
        got = from_pair[choose(n, back_add)].astype(jnp.float32)
        part = choose(n, back_part)
        dk = dk + got[:, :width]
        dv = dv + got[:, width:]
        parts[part, :, :width] = dk
        parts[part, :, width:] = dv
        out_buf[slot, :, :width] = dk.astype(jnp.bfloat16)
        out_buf[slot, :, width:] = dv.astype(jnp.bfloat16)
        at_step(n, back_after)
        return carry

    lax.fori_loop(0, len(BACK), return_step, 0)

    def finish_hub(k):
        at = 1 + HUBS.index(k)

        def add_pair():
            back_pair_copy(k).wait_recv()
            parts[at] += from_pair[k].astype(jnp.float32)

        if k < LINE:
            add_pair()
        else:
            pl.when(odd == 1)(add_pair)
        total = parts[at]
        for m, (step, held) in ROUTE.items():
            if held == k:
                back_line_copy(m).wait_recv()
                total = total + from_line[m].astype(jnp.float32)
        out_buf[2 * k] = total.astype(jnp.bfloat16)
        back_line_copy(k).start()

    finish_hub(HUBS[0])

    def query_tile(i):
        at = pl.ds(pl.multiple_of(i * COLS, COLS), COLS)
        part = jnp.dot(keys_t[...], dsc[:, at], preferred_element_type=jnp.float32)
        return (part * scale).T

    heads_tile = COLS // blk

    def far_rows(i, carry):
        part = query_tile((1 - core) * tiles + i).astype(jnp.bfloat16)
        for j in range(heads_tile):
            at = pl.ds(pl.multiple_of((i * heads_tile + j) * width, width), width)
            dq_send[:, at] = part[j * blk : (j + 1) * blk]
        return carry

    lax.fori_loop(0, tiles, far_rows, 0)
    dq_copy = copy(dq_send, dq_recv, core_send.at[3], core_recv.at[3], other_core)
    dq_copy.start()
    for k in HUBS[1:]:
        finish_hub(k)

    def near_rows(i, carry):
        part = query_tile(core * tiles + i)
        for j in range(heads_tile):
            at = pl.ds(pl.multiple_of((i * heads_tile + j) * width, width), width)
            near[:, at] = part[j * blk : (j + 1) * blk]
        return carry

    lax.fori_loop(0, tiles, near_rows, 0)
    dq_copy.wait()
    dq_ref[...] = (near[...] + dq_recv[...].astype(jnp.float32)).astype(jnp.bfloat16)

    @pl.when(odd == 0)
    def _():
        back_pair_copy(LINE).wait_recv()
        parts[0] += from_pair[LINE].astype(jnp.float32)

    total = parts[0]
    for k in (1, 8, 2, 6):
        back_line_copy(k).wait_recv()
        total = total + from_line[k].astype(jnp.float32)
    dk_ref[...] = total[:, :width].astype(jnp.bfloat16)
    dv_ref[...] = total[:, width:].astype(jnp.bfloat16)

    for k in range(1, LINE + 1):
        line_copy(k).wait_send()
        back_line_copy(k).wait_send()
        pair_copy(k).wait_send()
        back_pair_copy(k).wait_send()
    for c in core_copies():
        c.wait_send()


def hand_out(dq_ref, dk_ref, dv_ref, dq_out, dk_out, dv_out):
    dq_out[...] = dq_ref[...]
    dk_out[...] = dk_ref[...]
    dv_out[...] = dv_ref[...]


def solution(mesh):
    inner_count = mesh.shape["inner"]
    devices = inner_count * mesh.shape["outer"]

    def shards(queries, key_rows, value_rows, grad_output, doc_blocks):
        blk, width = key_rows.shape
        heads = queries.shape[1] // width
        rows = heads * blk
        bf16, f32 = jnp.bfloat16, jnp.float32
        vmem = pl.BlockSpec(memory_space=pltpu.VMEM)
        dma = pltpu.SemaphoreType.DMA
        grads = pl.pallas_call(
            functools.partial(kernel, inner_count, devices // 2, blk, width, heads),
            name="attention_backward",
            out_shape=(
                jax.ShapeDtypeStruct(queries.shape, bf16),
                jax.ShapeDtypeStruct(key_rows.shape, bf16),
                jax.ShapeDtypeStruct(value_rows.shape, bf16),
            ),
            in_specs=[pl.BlockSpec(memory_space=pl.ANY)] * 4 + [pl.BlockSpec(memory_space=pltpu.SMEM)],
            out_specs=(vmem, vmem, vmem),
            scratch_shapes=[
                pltpu.VMEM((SLOTS, blk, 2 * width), bf16),
                pltpu.VMEM((width, SLOTS * blk), bf16),
                pltpu.VMEM((2 * rows, width), bf16),
                pltpu.VMEM((2 * rows, width), bf16),
                pltpu.VMEM((width, 2 * rows), bf16),
                pltpu.VMEM((width, 2 * rows), bf16),
                pltpu.VMEM((SLOTS, blk, 2 * rows), f32),
                pltpu.VMEM((SLOTS, blk, 2 * rows), f32),
                pltpu.VMEM((SLOTS, 8, 2 * rows), f32),
                pltpu.VMEM((8, 2 * rows), f32),
                pltpu.VMEM((8, 2 * rows), f32),
                pltpu.VMEM((8, 2 * rows), f32),
                pltpu.VMEM((3, 2 * rows), f32),
                pltpu.VMEM((3, 2 * rows), f32),
                pltpu.VMEM((blk, 2 * rows), bf16),
                pltpu.VMEM((SLOTS * blk, 2 * rows), bf16),
                pltpu.VMEM((SLOTS, blk, 2 * width), bf16),
                pltpu.VMEM((LINE + 1, blk, 2 * width), bf16),
                pltpu.VMEM((LINE + 1, blk, 2 * width), bf16),
                pltpu.VMEM((len(HUBS) + 2, blk, 2 * width), f32),
                pltpu.VMEM((blk, heads * width), f32),
                pltpu.VMEM((blk, heads * width), bf16),
                pltpu.VMEM((blk, heads * width), bf16),
                dma((LINE + 1,)),
                dma((LINE + 1,)),
                dma((LINE + 1,)),
                dma((LINE + 1,)),
                dma((LINE + 1,)),
                dma((LINE + 1,)),
                dma((LINE + 1,)),
                dma((LINE + 1,)),
                dma((4,)),
                dma((4,)),
                dma((2 + 2 * heads,)),
            ],
            compiler_params=pltpu.CompilerParams(
                collective_id=0, has_side_effects=True, vmem_limit_bytes=56 << 20
            ),
        )(queries, key_rows, value_rows, grad_output, doc_blocks)
        return pl.pallas_call(
            hand_out,
            name="hand_out",
            out_shape=[jax.ShapeDtypeStruct(x.shape, x.dtype) for x in grads],
            in_specs=[vmem] * 3,
            out_specs=[vmem] * 3,
        )(*grads)

    rows = P(("outer", "inner"), None)
    return jax.shard_map(
        shards,
        mesh=mesh,
        in_specs=(rows, rows, rows, rows, P()),
        out_specs=(rows, rows, rows),
        check_vma=False,
    )
```

```python
import functools
import math

import jax
import jax.numpy as jnp
from jax import lax
from jax.experimental import pallas as pl
from jax.experimental.pallas import tpu as pltpu
from jax.sharding import PartitionSpec as P

MESH = pl.DeviceIdType.MESH
WINDOW = 16
LINE = WINDOW // 2
SLOTS = WINDOW + 1
COLS = 256
ROUTE = {
    1: (-1, 0),
    2: (-2, 0),
    8: (-8, 0),
    6: (-6, 0),
    4: (-2, 2),
    3: (-1, 2),
    7: (1, 8),
    5: (1, 6),
}
REACH = (1, 2, 6, 8)
HUBS = (6, 2, 8, 1)
BACK = (("other", 5), ("other", 4), ("other", 7), ("other", 3), ("other", 6))
BACK += (("other", 2), ("line", 5), ("line", 4), ("line", 7), ("line", 3))
BACK += (("other", 8), ("other", 1), ("line", 6), ("line", 2), ("line", 8))
BACK += (("line", 1), ("own", 0))
LOW = -1e30
HIGH = 3e38


def choose(n, values):
    out = values[0]
    for j in range(1, len(values)):
        out = jnp.where(n == j, values[j], out)
    return out


def at_step(n, actions):
    for j, one in actions.items():
        pl.when(n == j)(one)


def kernel(
    inner_count,
    chips,
    blk,
    width,
    heads,
    q_ref,
    k_ref,
    v_ref,
    do_ref,
    doc_ref,
    dq_ref,
    dk_ref,
    dv_ref,
    kv,
    keys_t,
    rows_q,
    rows_do,
    cols_q,
    cols_do,
    weights,
    dprobs,
    tile_max,
    run_max,
    run_sum,
    run_dot,
    own_stats,
    other_stats,
    low,
    dsc,
    out_buf,
    from_pair,
    from_line,
    parts,
    near,
    dq_send,
    dq_recv,
    line_send,
    line_recv,
    pair_send,
    pair_recv,
    back_line_send,
    back_line_recv,
    back_pair_send,
    back_pair_recv,
    core_send,
    core_recv,
    load_sem,
):
    rows = heads * blk
    tiles = rows // COLS
    both = 2 * tiles
    scale = width ** (-0.5)
    scale2 = scale * math.log2(math.e)
    per_group = inner_count // 2

    outer = lax.axis_index("outer")
    inner = lax.axis_index("inner")
    core = inner % 2
    chip = outer * per_group + inner // 2
    odd = chip % 2

    def device(chip_at, core_at):
        return {
            "outer": chip_at // per_group,
            "inner": (chip_at % per_group) * 2 + core_at,
        }

    def unit(k):
        return device((chip + 2 * k + chips) % chips, core)

    other_core = device(chip, 1 - core)
    pair = device(chip + 1 - 2 * odd, core)

    def copy(src, dst, send, recv, to):
        return pltpu.make_async_remote_copy(
            src_ref=src,
            dst_ref=dst,
            send_sem=send,
            recv_sem=recv,
            device_id=to,
            device_id_type=MESH,
        )

    def other(k):
        return 2 * k - 1 + 2 * odd if k < LINE else 2 * LINE - 1 - (2 * LINE - 2) * odd

    def line_copy(k):
        step, held = ROUTE[k]
        return copy(
            kv.at[2 * held], kv.at[2 * k], line_send.at[k], line_recv.at[k], unit(-step)
        )

    def pair_copy(k):
        src = 2 * k if k < LINE else 2 * LINE * odd
        dst = 2 * k + 1 - 2 * odd if k < LINE else 1 + (2 * LINE - 2) * odd
        return copy(
            kv.at[src], kv.at[dst], pair_send.at[k], pair_recv.at[k], pair
        )

    def pair_arrival(k):
        return copy(
            kv.at[0], kv.at[other(k)], pair_send.at[k], pair_recv.at[k], pair
        )

    def back_pair_copy(k):
        return copy(
            out_buf.at[other(k)], from_pair.at[k], back_pair_send.at[k],
            back_pair_recv.at[k], pair,
        )

    def back_line_copy(k):
        step, held = ROUTE[k]
        return copy(
            out_buf.at[2 * k], from_line.at[k], back_line_send.at[k],
            back_line_recv.at[k], unit(step),
        )

    def core_copies():
        own = pl.ds(pl.multiple_of(core * rows, rows), rows)
        return (
            copy(
                rows_q.at[own], rows_q.at[own], core_send.at[0], core_recv.at[0],
                other_core,
            ),
            copy(
                rows_do.at[own], rows_do.at[own], core_send.at[1], core_recv.at[1],
                other_core,
            ),
        )

    def core_arrivals():
        own = pl.ds(pl.multiple_of((1 - core) * rows, rows), rows)
        return (
            copy(
                rows_q.at[own], rows_q.at[own], core_send.at[0], core_recv.at[0],
                other_core,
            ),
            copy(
                rows_do.at[own], rows_do.at[own], core_send.at[1], core_recv.at[1],
                other_core,
            ),
        )

    barrier = pltpu.get_barrier_semaphore()
    for k in REACH:
        for to in (unit(k), unit(-k)):
            pl.semaphore_signal(barrier, inc=1, device_id=to, device_id_type=MESH)
    for to in (other_core, pair):
        pl.semaphore_signal(barrier, inc=1, device_id=to, device_id_type=MESH)

    loads = [
        pltpu.make_async_copy(k_ref, kv.at[0, :, pl.ds(0, width)], load_sem.at[0]),
        pltpu.make_async_copy(v_ref, kv.at[0, :, pl.ds(width, width)], load_sem.at[1]),
    ]
    for h in range(heads):
        at = pl.ds(pl.multiple_of(core * rows + h * blk, blk), blk)
        of = pl.ds(h * width, width)
        for j, (src, dst) in enumerate(((q_ref, rows_q), (do_ref, rows_do))):
            loads.append(
                pltpu.make_async_copy(
                    src.at[:, of], dst.at[at], load_sem.at[2 + 2 * h + j]
                )
            )
    for c in loads:
        c.start()
    run_max[...] = jnp.full(run_max.shape, LOW, jnp.float32)
    run_sum[...] = jnp.zeros(run_sum.shape, jnp.float32)
    run_dot[...] = jnp.zeros(run_dot.shape, jnp.float32)

    pl.semaphore_wait(barrier, 2 * len(REACH) + 2)

    def on_even(run):
        pl.when(odd == 0)(run)

    for c in loads[:2]:
        c.wait()
    for k in (6, 2, 8, 1):
        line_copy(k).start()
    on_even(lambda: pair_copy(LINE).start())
    for c in loads[2:]:
        c.wait()
    for c in core_copies():
        c.start()

    def columns(base):
        def one(i, carry):
            at = pl.ds(pl.multiple_of(base + i * blk, blk), blk)
            cols_q[:, at] = rows_q[at, :].T
            cols_do[:, at] = rows_do[at, :].T
            return carry

        lax.fori_loop(0, heads, one, 0)

    columns(core * rows)

    def pass_on(k):
        line_copy(k).wait_recv()
        for far, (step, held) in ROUTE.items():
            if held == k:
                line_copy(far).start()
        if k < LINE:
            pair_copy(k).start()
        else:
            pl.when(odd == 1)(lambda: pair_copy(k).start())

    pass_on(8)
    pass_on(2)
    for c in core_arrivals():
        c.wait_recv()
    columns((1 - core) * rows)
    pass_on(1)
    pass_on(6)

    def forward(slot, own):
        key_chip = (chip - slot + chips) % chips
        key_block = 2 * key_chip + core
        key_tag = doc_ref[key_block]
        key_tile = kv[slot, :, :width]
        value_tile = kv[slot, :, width:]
        keys_t[:, pl.ds(pl.multiple_of(slot * blk, blk), blk)] = key_tile.T

        def tile(i):
            at = pl.ds(i * COLS, COLS)
            query_half = i // tiles
            query_block = 2 * chip + query_half
            seen = (key_tag == doc_ref[query_block]) & (key_block <= query_block)
            s = jnp.dot(key_tile, cols_q[:, at], preferred_element_type=jnp.float32)
            dp = jnp.dot(value_tile, cols_do[:, at], preferred_element_type=jnp.float32)
            s = s * scale2
            if own:
                key_at = lax.broadcasted_iota(jnp.int32, (blk, COLS), 0)
                query_at = lax.broadcasted_iota(jnp.int32, (blk, COLS), 1) % blk
                s = jnp.where(
                    key_at - query_at <= (query_half - core) * blk, s, 2 * LOW
                )
            s3 = s.reshape(blk // 8, 8, COLS)
            dp3 = dp.reshape(blk // 8, 8, COLS)
            top = jnp.max(s3, axis=0)
            old = run_max[:, at]
            new = jnp.where(seen, jnp.maximum(old, top), old)
            used = jnp.where(seen, new, HIGH)
            w = jnp.exp2(s3 - used[None])
            factor = jnp.exp2(old - new)
            run_max[:, at] = new
            tile_max[slot, :, at] = new
            run_sum[:, at] = run_sum[:, at] * factor + jnp.sum(w, axis=0)
            run_dot[:, at] = run_dot[:, at] * factor + jnp.sum(w * dp3, axis=0)
            weights[slot, :, at] = w.reshape(blk, COLS)
            dprobs[slot, :, at] = dp

        for i in range(both):
            tile(i)

    forward(0, True)

    def take(*ks):
        def run():
            for k in ks:
                pass_on(k)

        return run

    def arrived(k):
        return lambda: pair_arrival(k).wait_recv()

    order = (16, 4, 12, 2, 14, 6, 10, 8, other(8), other(2), other(1), other(6))
    order += (other(7), other(3), other(5), other(4))
    before = {4: take(7), 5: take(3), 6: take(5, 4)}
    for j, k in ((8, 8), (9, 2), (10, 1), (11, 6), (12, 7), (13, 3), (14, 5), (15, 4)):
        before[j] = arrived(k)

    def gather_step(n, carry):
        at_step(n, before)
        forward(choose(n, order), False)
        return carry

    lax.fori_loop(0, len(order), gather_step, 0)

    m8 = run_max[...]
    m1 = jnp.max(m8, axis=0, keepdims=True)
    f8 = jnp.exp2(m8 - m1)
    own_stats[0:1, :] = m1
    own_stats[1:2, :] = jnp.sum(run_sum[...] * f8, axis=0, keepdims=True)
    own_stats[2:3, :] = jnp.sum(run_dot[...] * f8, axis=0, keepdims=True)
    stats_copy = copy(
        own_stats, other_stats, core_send.at[2], core_recv.at[2], other_core
    )
    stats_copy.start()
    stats_copy.wait()
    ma, mb = own_stats[0:1, :], other_stats[0:1, :]
    m1 = jnp.maximum(ma, mb)
    fa, fb = jnp.exp2(ma - m1), jnp.exp2(mb - m1)
    total = own_stats[1:2, :] * fa + other_stats[1:2, :] * fb
    delta = (own_stats[2:3, :] * fa + other_stats[2:3, :] * fb) / total
    run_max[...] = jnp.broadcast_to(m1, run_max.shape)
    run_sum[...] = jnp.broadcast_to(1.0 / total, run_sum.shape)
    run_dot[...] = jnp.broadcast_to(delta, run_dot.shape)

    def backward(slot):
        def tile(i):
            at = pl.ds(i * COLS, COLS)
            factor = jnp.exp2(tile_max[slot, :, at] - run_max[:, at]) * run_sum[:, at]
            p3 = weights[slot, :, at].reshape(blk // 8, 8, COLS) * factor[None]
            dp3 = dprobs[slot, :, at].reshape(blk // 8, 8, COLS)
            ds3 = p3 * (dp3 - run_dot[:, at][None])
            low[:, at] = p3.reshape(blk, COLS).astype(jnp.bfloat16)
            dsc[pl.ds(pl.multiple_of(slot * blk, blk), blk), at] = ds3.reshape(
                blk, COLS
            ).astype(jnp.bfloat16)

        for i in range(both):
            tile(i)
        dv = jnp.dot(low[...], rows_do[...], preferred_element_type=jnp.float32)
        dk = jnp.dot(
            dsc[pl.ds(pl.multiple_of(slot * blk, blk), blk), :],
            rows_q[...],
            preferred_element_type=jnp.float32,
        )
        return dk * scale, dv

    from_pair[0] = jnp.zeros(from_pair.shape[1:], jnp.bfloat16)

    def back_arrived(k):
        return lambda: back_pair_copy(k).wait_recv()

    def starts(copy_of, k):
        return lambda: copy_of(k).start()

    back_order = []
    back_add = []
    back_part = []
    back_before = {}
    back_after = {}
    for j, (kind, k) in enumerate(BACK):
        back_order.append(other(k) if kind == "other" else 2 * k)
        back_add.append(0)
        back_part.append(len(HUBS) + 1)
        if kind == "other":
            back_after[j] = starts(back_pair_copy, k)
        elif kind == "own":
            back_part[j] = 0
        elif k in HUBS:
            back_part[j] = 1 + HUBS.index(k)
        else:
            back_add[j] = k
            back_before[j] = back_arrived(k)
            back_after[j] = starts(back_line_copy, k)

    def return_step(n, carry):
        slot = choose(n, back_order)
        dk, dv = backward(slot)
        at_step(n, back_before)
        got = from_pair[choose(n, back_add)].astype(jnp.float32)
        part = choose(n, back_part)
        dk = dk + got[:, :width]
        dv = dv + got[:, width:]
        parts[part, :, :width] = dk
        parts[part, :, width:] = dv
        out_buf[slot, :, :width] = dk.astype(jnp.bfloat16)
        out_buf[slot, :, width:] = dv.astype(jnp.bfloat16)
        at_step(n, back_after)
        return carry

    lax.fori_loop(0, len(BACK), return_step, 0)

    def finish_hub(k):
        at = 1 + HUBS.index(k)

        def add_pair():
            back_pair_copy(k).wait_recv()
            parts[at] += from_pair[k].astype(jnp.float32)

        if k < LINE:
            add_pair()
        else:
            pl.when(odd == 1)(add_pair)
        total = parts[at]
        for m, (step, held) in ROUTE.items():
            if held == k:
                back_line_copy(m).wait_recv()
                total = total + from_line[m].astype(jnp.float32)
        out_buf[2 * k] = total.astype(jnp.bfloat16)
        back_line_copy(k).start()

    finish_hub(HUBS[0])

    def query_tile(i):
        at = pl.ds(pl.multiple_of(i * COLS, COLS), COLS)
        part = jnp.dot(keys_t[...], dsc[:, at], preferred_element_type=jnp.float32)
        return (part * scale).T

    heads_tile = COLS // blk

    def far_rows(i, carry):
        part = query_tile((1 - core) * tiles + i).astype(jnp.bfloat16)
        for j in range(heads_tile):
            at = pl.ds(pl.multiple_of((i * heads_tile + j) * width, width), width)
            dq_send[:, at] = part[j * blk : (j + 1) * blk]
        return carry

    lax.fori_loop(0, tiles, far_rows, 0)
    dq_copy = copy(dq_send, dq_recv, core_send.at[3], core_recv.at[3], other_core)
    dq_copy.start()
    for k in HUBS[1:]:
        finish_hub(k)

    def near_rows(i, carry):
        part = query_tile(core * tiles + i)
        for j in range(heads_tile):
            at = pl.ds(pl.multiple_of((i * heads_tile + j) * width, width), width)
            near[:, at] = part[j * blk : (j + 1) * blk]
        return carry

    lax.fori_loop(0, tiles, near_rows, 0)
    dq_copy.wait()
    dq_ref[...] = (near[...] + dq_recv[...].astype(jnp.float32)).astype(jnp.bfloat16)

    @pl.when(odd == 0)
    def _():
        back_pair_copy(LINE).wait_recv()
        parts[0] += from_pair[LINE].astype(jnp.float32)

    total = parts[0]
    for k in (1, 8, 2, 6):
        back_line_copy(k).wait_recv()
        total = total + from_line[k].astype(jnp.float32)
    dk_ref[...] = total[:, :width].astype(jnp.bfloat16)
    dv_ref[...] = total[:, width:].astype(jnp.bfloat16)

    for k in range(1, LINE + 1):
        line_copy(k).wait_send()
        back_line_copy(k).wait_send()
        pair_copy(k).wait_send()
        back_pair_copy(k).wait_send()
    for c in core_copies():
        c.wait_send()


def hand_out(dq_ref, dk_ref, dv_ref, dq_out, dk_out, dv_out):
    dq_out[...] = dq_ref[...]
    dk_out[...] = dk_ref[...]
    dv_out[...] = dv_ref[...]


def solution(mesh):
    inner_count = mesh.shape["inner"]
    devices = inner_count * mesh.shape["outer"]

    def shards(queries, key_rows, value_rows, grad_output, doc_blocks):
        blk, width = key_rows.shape
        heads = queries.shape[1] // width
        rows = heads * blk
        bf16, f32 = jnp.bfloat16, jnp.float32
        vmem = pl.BlockSpec(memory_space=pltpu.VMEM)
        dma = pltpu.SemaphoreType.DMA
        grads = pl.pallas_call(
            functools.partial(kernel, inner_count, devices // 2, blk, width, heads),
            name="attention_backward",
            out_shape=(
                jax.ShapeDtypeStruct(queries.shape, bf16),
                jax.ShapeDtypeStruct(key_rows.shape, bf16),
                jax.ShapeDtypeStruct(value_rows.shape, bf16),
            ),
            in_specs=[pl.BlockSpec(memory_space=pl.ANY)] * 4 + [pl.BlockSpec(memory_space=pltpu.SMEM)],
            out_specs=(vmem, vmem, vmem),
            scratch_shapes=[
                pltpu.VMEM((SLOTS, blk, 2 * width), bf16),
                pltpu.VMEM((width, SLOTS * blk), bf16),
                pltpu.VMEM((2 * rows, width), bf16),
                pltpu.VMEM((2 * rows, width), bf16),
                pltpu.VMEM((width, 2 * rows), bf16),
                pltpu.VMEM((width, 2 * rows), bf16),
                pltpu.VMEM((SLOTS, blk, 2 * rows), f32),
                pltpu.VMEM((SLOTS, blk, 2 * rows), f32),
                pltpu.VMEM((SLOTS, 8, 2 * rows), f32),
                pltpu.VMEM((8, 2 * rows), f32),
                pltpu.VMEM((8, 2 * rows), f32),
                pltpu.VMEM((8, 2 * rows), f32),
                pltpu.VMEM((3, 2 * rows), f32),
                pltpu.VMEM((3, 2 * rows), f32),
                pltpu.VMEM((blk, 2 * rows), bf16),
                pltpu.VMEM((SLOTS * blk, 2 * rows), bf16),
                pltpu.VMEM((SLOTS, blk, 2 * width), bf16),
                pltpu.VMEM((LINE + 1, blk, 2 * width), bf16),
                pltpu.VMEM((LINE + 1, blk, 2 * width), bf16),
                pltpu.VMEM((len(HUBS) + 2, blk, 2 * width), f32),
                pltpu.VMEM((blk, heads * width), f32),
                pltpu.VMEM((blk, heads * width), bf16),
                pltpu.VMEM((blk, heads * width), bf16),
                dma((LINE + 1,)),
                dma((LINE + 1,)),
                dma((LINE + 1,)),
                dma((LINE + 1,)),
                dma((LINE + 1,)),
                dma((LINE + 1,)),
                dma((LINE + 1,)),
                dma((LINE + 1,)),
                dma((4,)),
                dma((4,)),
                dma((2 + 2 * heads,)),
            ],
            compiler_params=pltpu.CompilerParams(
                collective_id=0, has_side_effects=True, vmem_limit_bytes=56 << 20
            ),
        )(queries, key_rows, value_rows, grad_output, doc_blocks)
        return pl.pallas_call(
            hand_out,
            name="hand_out",
            out_shape=[jax.ShapeDtypeStruct(x.shape, x.dtype) for x in grads],
            in_specs=[vmem] * 3,
            out_specs=[vmem] * 3,
        )(*grads)

    rows = P(("outer", "inner"), None)
    return jax.shard_map(
        shards,
        mesh=mesh,
        in_specs=(rows, rows, rows, rows, P()),
        out_specs=(rows, rows, rows),
        check_vma=False,
    )
```
